32 devices in a mesh: seq: 8 (over y, x, core), head: 4 (over z).
Axes of the slice: x: 2, y: 2, z: 4, core: 2. Of those that a mesh axis runs over, the one named last changes fastest.
Arguments:
- queries: bfloat16 [1280, 64, 128], P(('seq', 'head')), may hold values from -8 to 8
- key_one: bfloat16 [1280, 128], P(('seq', 'head')), may hold values from -6 to 6
- value_one: bfloat16 [1280, 128], P(('seq', 'head')), may hold values from -6 to 6
- key_two: bfloat16 [1280, 128], P(('seq', 'head')), may hold values from -6 to 6
- value_two: bfloat16 [1280, 128], P(('seq', 'head')), may hold values from -6 to 6
Outputs:
- attended: bfloat16 [1280, 64, 128], P(('seq', 'head'))
The draws below stay inside these ranges and needn't reach their ends.
All inputs are finite; a program needn't handle non-finite values.
Results may differ from the reference program's by a relative error of at most 0.0058.
Values may be sent and summed in bfloat16 or wider, within the bound.
A program may use at most 64 MiB of HBM per device.

```python
import math
import jax
import jax.numpy as jnp
from jax import lax

HEADS = 64
HEAD_DIM = 128
WIN_ONE = 512
WIN_TWO = 32
SEQ_LEN = 1280


def base_rows(key, shape):
    return jnp.clip(jax.random.normal(key, shape, jnp.float32), -6.0, 6.0)


def draw_key_one(key, part):
    key_rows = base_rows(jax.random.fold_in(key, 11), (SEQ_LEN, HEAD_DIM))
    return key_rows.astype(jnp.bfloat16)


def draw_key_two(key, part):
    key_rows = base_rows(jax.random.fold_in(key, 13), (SEQ_LEN, HEAD_DIM))
    return key_rows.astype(jnp.bfloat16)


def draw_queries(key, part):
    query_rows = base_rows(jax.random.fold_in(key, 17), (SEQ_LEN, HEADS, HEAD_DIM))
    return query_rows.astype(jnp.bfloat16)


def block_scale(stream_key, dims, split, low, high):
    def one(dim, shards_of):
        steps = jax.random.uniform(jax.random.fold_in(jax.random.fold_in(stream_key, 6), dim), (shards_of,), jnp.float32, low / len(split), high / len(split))
        return jnp.repeat(jnp.exp(steps), dims[dim] // shards_of).reshape((-1,) + (1,) * (len(dims) - dim - 1))

    gain = one(*split[0])
    for cut in split[1:]:
        gain = gain * one(*cut)
    return gain


def normal_values(rng, shape, spread, most, cuts=(), kind=jnp.bfloat16):
    gain = block_scale(rng, shape, cuts, -0.22, 0.18) if cuts else 1.0
    drawn = jax.random.normal(rng, shape, jnp.float32) * spread * gain
    return jnp.minimum(jnp.maximum(drawn, -most), most).astype(kind)


def setup_inputs(seed: int = 0) -> dict:
    arg_keys = jax.random.split(jax.random.key(seed), 6)
    return {
        "queries": draw_queries(jax.random.fold_in(arg_keys[5], 71), 0),
        "key_one": draw_key_one(jax.random.fold_in(arg_keys[5], 71), 0),
        "value_one": normal_values(arg_keys[2], (SEQ_LEN, HEAD_DIM), 1.0, 6.0, ((0, 32),)),
        "key_two": draw_key_two(jax.random.fold_in(arg_keys[5], 71), 0),
        "value_two": normal_values(arg_keys[4], (SEQ_LEN, HEAD_DIM), 1.0, 6.0, ((0, 32),)),
    }


def window_attend(query_rows, keys_one, values_one, keys_two, values_two, first_pos):
    block_rows, group_size, head_depth = query_rows.shape
    width_two = keys_two.shape[0] - block_rows + 1
    width_one = keys_one.shape[0] - block_rows + 1
    key_span = keys_one.shape[0]
    near_keys = jnp.stack([keys_two[width_two - 1 - offset:width_two - 1 - offset + block_rows] for offset in range(width_two)], axis=1)
    near_values = jnp.stack([values_two[width_two - 1 - offset:width_two - 1 - offset + block_rows] for offset in range(width_two)], axis=1)
    score_scale = 1.0 / math.sqrt(head_depth)
    product = (query_rows.astype(jnp.float32)[:, :, None, :] * near_keys.astype(jnp.float32)[:, None, :, :] * score_scale).astype(jnp.bfloat16)
    logits = lax.dot_general(product.reshape(-1, head_depth), keys_one, (((1,), (1,)), ((), ())), preferred_element_type=jnp.float32)
    logits = logits.reshape(block_rows, group_size, width_two, key_span)
    row_pos = lax.broadcasted_iota(jnp.int32, (block_rows, 1, 1, 1), 0)
    lag_pos = lax.broadcasted_iota(jnp.int32, (1, 1, width_two, 1), 2)
    col_pos = lax.broadcasted_iota(jnp.int32, (1, 1, 1, key_span), 3)
    inside = (col_pos >= row_pos) & (col_pos <= row_pos + width_one - 1)
    inside = inside & (first_pos - width_one + 1 + col_pos >= 0) & (first_pos + row_pos - lag_pos >= 0)
    logits = jnp.where(inside, logits, -1e+30)
    peak_value = lax.optimization_barrier(jnp.max(logits, axis=(2, 3), keepdims=True))
    raised = jnp.exp(logits - peak_value)
    weights = (raised / lax.optimization_barrier(jnp.sum(raised, axis=(2, 3), keepdims=True))).astype(jnp.bfloat16)
    blended = jnp.dot(weights.reshape(-1, key_span), values_one, preferred_element_type=jnp.float32)
    blended = blended.reshape(block_rows, group_size, width_two, head_depth)
    return lax.optimization_barrier(jnp.sum(blended * near_values.astype(jnp.float32)[:, None, :, :], axis=2))

def reference(queries, key_one, value_one, key_two, value_two):
    total_rows, head_count, head_depth = queries.shape
    block_rows = math.gcd(total_rows, 16)
    zeros_one = jnp.zeros((WIN_ONE - 1, head_depth), key_one.dtype)
    zeros_two = jnp.zeros((WIN_TWO - 1, head_depth), key_two.dtype)
    long_keys_one = jnp.concatenate([zeros_one, key_one], axis=0)
    long_values_one = jnp.concatenate([zeros_one, value_one], axis=0)
    long_keys_two = jnp.concatenate([zeros_two, key_two], axis=0)
    long_values_two = jnp.concatenate([zeros_two, value_two], axis=0)

    def attend(index):
        start = (index * block_rows).astype(jnp.int32)
        query_rows = lax.dynamic_slice_in_dim(queries, start, block_rows, 0)
        keys_one = lax.dynamic_slice_in_dim(long_keys_one, start, block_rows + WIN_ONE - 1, 0)
        values_one = lax.dynamic_slice_in_dim(long_values_one, start, block_rows + WIN_ONE - 1, 0)
        keys_two = lax.dynamic_slice_in_dim(long_keys_two, start, block_rows + WIN_TWO - 1, 0)
        values_two = lax.dynamic_slice_in_dim(long_values_two, start, block_rows + WIN_TWO - 1, 0)
        return window_attend(query_rows, keys_one, values_one, keys_two, values_two, start).astype(jnp.bfloat16)
    blocks = lax.map(attend, jnp.arange(total_rows // block_rows, dtype=jnp.int32))
    return blocks.reshape(total_rows, head_count, head_depth)
```

```python
import functools
import math

import jax
import jax.numpy as jnp
from jax import lax
from jax.experimental import pallas as pl
from jax.experimental.pallas import tpu as pltpu
from jax.sharding import PartitionSpec as P

WIN_ONE = 512
WIN_TWO = 32
LAG_CHUNK = 8
ROW_L = 1
SAFE = 100.0


def pieces_behind(window, rows):
    return (window - 1) // rows + 1


def shards_behind(reach, inner):
    return (reach + inner - 1) // inner


def halo_kernel(reach, k1, v1, k2, v2, k1_out, v1_out, k2_out, v2_out, *sems):
    side_send, side_recv, fore_send, fore_recv, near_send, near_recv = sems
    inner, outer = lax.axis_size("head"), lax.axis_size("seq")
    seq, col = lax.axis_index("seq"), lax.axis_index("head")
    me, count = seq * inner + col, outer * inner
    shards = shards_behind(reach[0], inner)
    base = shards * inner
    firsts = ((k1, k1_out), (v1, v1_out))
    seconds = ((k2, k2_out), (v2, v2_out))

    def remote(source, target, send, recv, where):
        return pltpu.make_async_remote_copy(
            src_ref=source,
            dst_ref=target,
            send_sem=send,
            recv_sem=recv,
            device_id=where,
            device_id_type=pl.DeviceIdType.MESH,
        )

    def around(turn):
        return (col + turn) % inner

    def side(turn):
        return [
            remote(
                source,
                target.at[base + col],
                side_send.at[flow, turn - 1],
                side_recv.at[flow, turn - 1],
                (seq, around(turn)),
            )
            for flow, (source, target) in enumerate(firsts)
        ]

    def side_arrival(turn):
        return [
            remote(
                source,
                target.at[base + around(turn)],
                side_send.at[flow, inner - turn - 1],
                side_recv.at[flow, inner - turn - 1],
                (seq, around(turn)),
            )
            for flow, (source, target) in enumerate(firsts)
        ]

    def fore(hop, turn):
        return [
            remote(
                source if turn == 0 else target.at[base + around(turn)],
                target.at[(shards - hop) * inner + around(turn)],
                fore_send.at[flow, hop - 1, turn],
                fore_recv.at[flow, hop - 1, turn],
                (seq + hop, col),
            )
            for flow, (source, target) in enumerate(firsts)
        ]

    def near(step):
        there = me + step
        return [
            remote(
                source,
                target.at[reach[1] - step],
                near_send.at[flow, step - 1],
                near_recv.at[flow, step - 1],
                (there // inner, there % inner),
            )
            for flow, (source, target) in enumerate(seconds)
        ]

    def wanted(hop, turn):
        return hop * inner <= reach[0] + around(turn) - col

    def greet(where):
        pl.semaphore_signal(barrier, inc=1, device_id=where, device_id_type=pl.DeviceIdType.MESH)

    barrier = pltpu.get_barrier_semaphore()
    hops = (reach[0] + inner - 1 - col) // inner
    for turn in range(1, inner):
        greet((seq, around(turn)))
    for hop in range(1, shards + 1):

        @pl.when((seq - hop >= 0) & (hop <= hops))
        def _():
            greet((seq - hop, col))

    for step in range(1, reach[1] + 1):

        @pl.when(me - step >= 0)
        def _():
            greet(((me - step) // inner, (me - step) % inner))

    peers = inner - 1 + jnp.minimum(hops, outer - 1 - seq) + jnp.minimum(reach[1], count - 1 - me)
    pl.semaphore_wait(barrier, peers)

    for turn in range(1, inner):
        for copy in side(turn):
            copy.start()
    for turn in range(inner):
        if turn:
            for copy in side_arrival(turn):
                copy.wait_recv()
        for hop in range(shards, 0, -1):

            @pl.when((seq + hop < outer) & wanted(hop, turn))
            def _():
                for copy in fore(hop, turn):
                    copy.start()

        if turn == 0:
            for step in range(1, reach[1] + 1):

                @pl.when(me + step < count)
                def _():
                    for copy in near(step):
                        copy.start()

    for turn in range(inner):
        for hop in range(shards, 0, -1):

            @pl.when((seq - hop >= 0) & wanted(hop, turn))
            def _():
                for copy in fore(hop, turn):
                    copy.wait_recv()

            @pl.when((seq + hop < outer) & wanted(hop, turn))
            def _():
                for copy in fore(hop, turn):
                    copy.wait_send()

    for step in range(1, reach[1] + 1):

        @pl.when(me - step >= 0)
        def _():
            for copy in near(step):
                copy.wait_recv()

        @pl.when(me + step < count)
        def _():
            for copy in near(step):
                copy.wait_send()

    for turn in range(1, inner):
        for copy in side(turn):
            copy.wait_send()


def attend_kernel(*refs):
    q_far, far, out, q, near, fetched = refs[0], refs[1:9], refs[9], refs[10], refs[11:19], refs[19]
    k1f, v1f, k2f, v2f, kw, vt, vold, vnew, spread2, num_ref, den_ref, raised, scores = refs[20:]
    piece, heads, depth = q.shape
    inner = lax.axis_size("head")
    reach = near[0].shape[0]
    skip = lax.axis_index("head") + shards_behind(reach, inner) * inner - reach
    far = [far[0].at[pl.ds(skip, reach)], far[1].at[pl.ds(skip, reach)], *far[2:]]
    fetches = [
        pltpu.make_async_copy(source, target, fetched.at[index])
        for index, (source, target) in enumerate(zip(far, near))
    ]
    early = pltpu.make_async_copy(q_far.at[pl.ds(0, 1)], q.at[pl.ds(0, 1)], fetched.at[8])
    rest = pltpu.make_async_copy(q_far.at[pl.ds(1, piece - 1)], q.at[pl.ds(1, piece - 1)], fetched.at[9])
    for fetch in fetches:
        fetch.start()
    early.start()
    rest.start()
    k1h, v1h, k2h, v2h, k1, v1, k2, v2 = near
    for fetch in fetches:
        fetch.wait()
    me = lax.axis_index("seq") * inner + lax.axis_index("head")
    lead_one = k1h.shape[0] * piece
    lead_two = k2h.shape[0] * piece
    scale = math.log2(math.e) / math.sqrt(depth)

    def spread(target, behind, own):
        for slot in range(behind.shape[0]):
            target[slot * piece : (slot + 1) * piece, :] = behind[slot].astype(jnp.float32)
        lead = behind.shape[0] * piece
        target[lead : lead + piece, :] = own[...].astype(jnp.float32)
        if lead + piece < target.shape[0]:
            target[lead + piece :, :] = jnp.zeros((target.shape[0] - lead - piece, depth), jnp.float32)

    spread(k1f, k1h, k1)
    spread(v1f, v1h, v1)
    spread(k2f, k2h, k2)
    spread(v2f, v2h, v2)
    first_one = lead_one - me * piece
    first_two = lead_two - me * piece

    @pl.when(first_one > 0)
    def _():
        pos = lax.broadcasted_iota(jnp.int32, k1f.shape, 0)
        whole = k1f[...]
        head_row = jnp.sum(jnp.where(pos == first_one, whole, 0.0), axis=0, keepdims=True)
        k1f[...] = jnp.where(pos < first_one, head_row, whole)
        v1f[...] = jnp.where(pos < first_one, 0.0, v1f[...])

    pos_two = lax.broadcasted_iota(jnp.int32, k2f.shape, 0)
    whole_two = k2f[...]
    head_two = jnp.sum(jnp.where(pos_two == first_two, whole_two, 0.0), axis=0, keepdims=True)
    k2f[...] = jnp.where(pos_two < first_two, head_two, whole_two) * scale
    pos_v = lax.broadcasted_iota(jnp.int32, v2f.shape, 0)
    v2f[...] = jnp.where(pos_v < first_two, 0.0, v2f[...])

    span = LAG_CHUNK * heads
    chunks = WIN_TWO // LAG_CHUNK
    start_one = lead_one - WIN_ONE
    fresh = -(-piece // 16) * 16
    lane = lax.broadcasted_iota(jnp.int32, (depth + 16, depth), 1)
    sub = lax.broadcasted_iota(jnp.int32, (depth + 16, depth), 0)
    row_f = lax.broadcasted_iota(jnp.int32, (fresh, depth), 0)

    kw[...] = k1f[start_one : start_one + WIN_ONE, :].astype(jnp.bfloat16)
    for lo in range(0, WIN_ONE, depth):
        turned = jnp.transpose(v1f[start_one + lo : start_one + lo + depth, :])
        valid = jnp.where(lane[depth:] + (start_one + lo) < first_one, 0.0, 1.0)
        made = jnp.concatenate([turned, valid], axis=0)
        if lo == 0:
            vold[...] = made
        else:
            vt[:, lo : lo + depth] = made.astype(jnp.bfloat16)
    vnew[...] = jnp.concatenate(
        [jnp.transpose(v1f[lead_one : lead_one + depth, :]), jnp.ones((16, depth), jnp.float32)], axis=0
    )

    def load_keys(token):
        head = jnp.where(row_f <= token, k1f[lead_one : lead_one + fresh, :], k1f[start_one : start_one + fresh, :])
        kw[:fresh, :] = head.astype(jnp.bfloat16)

    def load_values(token):
        vt[:, :depth] = jnp.where(lane <= token, vnew[...], vold[...]).astype(jnp.bfloat16)

    behind_two = WIN_TWO - 1

    def spread_values(index):
        row = lead_two - behind_two + index
        late = jnp.broadcast_to(v2f[pl.ds(row + 1, 1), :], (heads, depth))
        soon = jnp.broadcast_to(v2f[pl.ds(row, 1), :], (heads, depth))
        spread2[index] = jnp.transpose(jnp.concatenate([late, soon], axis=0))

    own = jnp.where(lane[:depth] == sub[:depth], 1.0, 0.0).astype(jnp.bfloat16)
    for index in range(0, behind_two - 1, 2):
        rows = []
        for at in (index, index + 1):
            row = lead_two - behind_two + at
            rows.append(jnp.broadcast_to(v2f[row + 1 : row + 2, :], (heads, depth)))
            rows.append(jnp.broadcast_to(v2f[row : row + 1, :], (heads, depth)))
        made = lax.dot_general(
            own,
            jnp.concatenate(rows, axis=0).astype(jnp.bfloat16),
            (((1,), (1,)), ((), ())),
            preferred_element_type=jnp.float32,
        )
        spread2[index] = made[:, :depth]
        spread2[index + 1] = made[:, depth:]

    def products(token, chunk):
        query = q[token].astype(jnp.float32)
        rows = []
        for lag in range(chunk * LAG_CHUNK, (chunk + 1) * LAG_CHUNK):
            near = k2f[pl.ds(lead_two + token - lag, 1), :]
            rows.append((query * near).astype(jnp.bfloat16))
        return jnp.concatenate(rows, axis=0)

    def logits(token, chunk, top):
        product = products(token, chunk)
        for lo in range(0, WIN_ONE, WIN_ONE // ROW_L):
            made = lax.dot_general(
                kw[lo : lo + WIN_ONE // ROW_L, :],
                product,
                (((1,), (1,)), ((), ())),
                preferred_element_type=jnp.float32,
            )
            scores[lo : lo + WIN_ONE // ROW_L, chunk * span : (chunk + 1) * span] = made
            best = jnp.max(made.reshape(WIN_ONE // ROW_L // 8, 8, span), axis=0)
            parts = [best[:, at : at + depth] for at in range(0, span, depth)]
            top = parts if top is None else [jnp.maximum(a, b) for a, b in zip(top, parts)]
        return top

    num_ref[...] = jnp.zeros(num_ref.shape, jnp.float32)
    den_ref[...] = jnp.ones(den_ref.shape, jnp.float32)

    def finish(token, num, den):
        den = den + pltpu.roll(den, heads, 1)
        inverse = 1.0 / den
        num = num.reshape(depth // 8, 8, depth) * inverse[None]
        turned = jnp.transpose(num.reshape(depth, depth))
        out[token] = (turned[:heads] + turned[heads:]).astype(out.dtype)

    def weigh(chunk, peak):
        parts = scores[:, chunk * span : (chunk + 1) * span].reshape(WIN_ONE // 8, 8, span)
        raised[chunk] = jnp.exp2(parts - peak[None]).astype(jnp.bfloat16).reshape(WIN_ONE, span)

    def blend(token, chunk, num, den):
        mixed = jnp.dot(vt[...], raised[chunk], preferred_element_type=jnp.float32)
        for at in range(0, span, depth):
            lag = chunk * LAG_CHUNK + at // heads
            more = mixed[:depth, at : at + depth] * spread2[token - lag + behind_two - 1]
            known = jnp.where(lane[:8] // heads + (lag - token) <= me * piece, 1.0, 0.0)
            count = mixed[depth : depth + 8, at : at + depth] * known
            num = more if num is None else num + more
            den = count if den is None else den + count
        return num, den

    def last_blend(token):
        num, den = blend(token, chunks - 1, num_ref[...], den_ref[...])
        finish(token, num, den)

    def step(token, top):
        later = jnp.minimum(token + 1, piece - 1)
        peak = jnp.max(functools.reduce(jnp.maximum, top), axis=0, keepdims=True)
        peak = jnp.broadcast_to(jnp.maximum(peak, pltpu.roll(peak, heads, 1)), (8, depth))
        peak = jnp.concatenate([peak] * (span // depth), axis=1)
        last_blend(jnp.maximum(token - 1, 0))
        load_values(token)
        load_keys(later)
        spread_values(token + behind_two - 1)
        num = den = later_top = None
        for chunk in range(chunks):
            if chunk:
                num, den = blend(token, chunk - 1, num, den)
            weigh(chunk, peak)
            later_top = logits(later, chunk, later_top)
        num_ref[...] = num
        den_ref[...] = den
        return later_top

    def plain(token, chunk):
        raised[chunk] = jnp.exp2(
            lax.dot_general(
                kw[...], products(token, chunk), (((1,), (1,)), ((), ())), preferred_element_type=jnp.float32
            )
        ).astype(jnp.bfloat16)

    def quick(token, carry):
        last_blend(jnp.maximum(token - 1, 0))
        load_values(token)
        load_keys(token)
        spread_values(token + behind_two - 1)
        num = den = None
        for chunk in range(chunks):
            plain(token, chunk)
            if chunk:
                num, den = blend(token, chunk - 1, num, den)
        num_ref[...] = num
        den_ref[...] = den
        return carry

    def limit_squared():
        most = jnp.max(jnp.abs(q[...].astype(jnp.float32)), axis=1)
        most = (most * most).astype(jnp.bfloat16)
        twos = k2f[...]
        twos = (twos * twos).astype(jnp.bfloat16)
        ones = k1f[...]
        ones = (ones * ones).astype(jnp.bfloat16)
        over = (((1,), (1,)), ((), ()))
        left = lax.dot_general(most, twos, over, preferred_element_type=jnp.float32)
        right = lax.dot_general(
            ones, jnp.ones((depth, depth), jnp.bfloat16), over, preferred_element_type=jnp.float32
        )
        return 1.05 * jnp.max(left) * jnp.max(right)

    def shifted():
        load_keys(0)
        top = None
        for chunk in range(chunks):
            top = logits(0, chunk, top)
        lax.fori_loop(0, piece, step, top)

    def plainly():
        lax.fori_loop(0, piece, quick, 0)

    early.wait()
    rest.wait()
    small = limit_squared() < SAFE * SAFE

    @pl.when(small)
    def _():
        plainly()

    @pl.when(jnp.logical_not(small))
    def _():
        shifted()

    last_blend(piece - 1)


def body(queries, key_one, value_one, key_two, value_two):
    piece, heads, depth = queries.shape
    reach = (pieces_behind(WIN_ONE, piece), pieces_behind(WIN_TWO, piece))
    anywhere = pl.BlockSpec(memory_space=pl.ANY)
    vmem = pl.BlockSpec(memory_space=pltpu.VMEM)
    inner = lax.axis_size("head")
    shards = shards_behind(reach[0], inner)
    slots = (shards + 1) * inner
    behind = [jax.ShapeDtypeStruct((r, piece, depth), key_one.dtype) for r in (slots, slots, reach[1], reach[1])]
    windows = [jax.ShapeDtypeStruct((r, piece, depth), key_one.dtype) for r in (reach[0], reach[0], reach[1], reach[1])]
    halos = pl.pallas_call(
        functools.partial(halo_kernel, reach),
        out_shape=behind,
        in_specs=[anywhere] * 4,
        out_specs=[anywhere] * 4,
        scratch_shapes=[
            *[pltpu.SemaphoreType.DMA((2, inner))] * 2,
            *[pltpu.SemaphoreType.DMA((2, shards, inner))] * 2,
            *[pltpu.SemaphoreType.DMA((2, reach[1]))] * 2,
        ],
        compiler_params=pltpu.CompilerParams(collective_id=0, has_side_effects=True),
    )(key_one, value_one, key_two, value_two)
    long_one = (reach[0] * piece + depth, depth)
    long_two = (reach[1] * piece + depth, depth)
    return pl.pallas_call(
        attend_kernel,
        out_shape=jax.ShapeDtypeStruct(queries.shape, queries.dtype),
        in_specs=[anywhere] * 9,
        out_specs=vmem,
        scratch_shapes=[
            pltpu.VMEM(queries.shape, queries.dtype),
            *[pltpu.VMEM(x.shape, x.dtype) for x in (*windows, key_one, value_one, key_two, value_two)],
            pltpu.SemaphoreType.DMA((10,)),
            pltpu.VMEM(long_one, jnp.float32),
            pltpu.VMEM(long_one, jnp.float32),
            pltpu.VMEM(long_two, jnp.float32),
            pltpu.VMEM(long_two, jnp.float32),
            pltpu.VMEM((WIN_ONE, depth), jnp.bfloat16),
            pltpu.VMEM((depth + 16, WIN_ONE), jnp.bfloat16),
            pltpu.VMEM((depth + 16, depth), jnp.float32),
            pltpu.VMEM((depth + 16, depth), jnp.float32),
            pltpu.VMEM((piece + WIN_TWO - 2, depth, depth), jnp.float32),
            pltpu.VMEM((depth, depth), jnp.float32),
            pltpu.VMEM((8, depth), jnp.float32),
            pltpu.VMEM((WIN_TWO // LAG_CHUNK, WIN_ONE, LAG_CHUNK * heads), jnp.bfloat16),
            pltpu.VMEM((WIN_ONE, WIN_TWO * heads), jnp.float32),
        ],
    )(queries, *halos, key_one, value_one, key_two, value_two)


def solution(mesh):
    rows = P(("seq", "head"), None)
    placed = (P(("seq", "head"), None, None), rows, rows, rows, rows)
    return jax.shard_map(
        body, mesh=mesh, in_specs=placed, out_specs=P(("seq", "head"), None, None), check_vma=False
    )
```

```python
import functools
import math

import jax
import jax.numpy as jnp
from jax import lax
from jax.experimental import pallas as pl
from jax.experimental.pallas import tpu as pltpu
from jax.sharding import PartitionSpec as P

WIN_ONE = 512
WIN_TWO = 32
LAG_CHUNK = 8
ROW_L = 1
SAFE = 100.0
UNROLL = 8


def pieces_behind(window, rows):
    return (window - 1) // rows + 1


def shards_behind(reach, inner):
    return (reach + inner - 1) // inner


def halo_kernel(reach, k1, v1, k2, v2, k1_out, v1_out, k2_out, v2_out, *sems):
    side_send, side_recv, fore_send, fore_recv, near_send, near_recv = sems
    inner, outer = lax.axis_size("head"), lax.axis_size("seq")
    seq, col = lax.axis_index("seq"), lax.axis_index("head")
    me, count = seq * inner + col, outer * inner
    shards = shards_behind(reach[0], inner)
    base = shards * inner
    firsts = ((k1, k1_out), (v1, v1_out))
    seconds = ((k2, k2_out), (v2, v2_out))

    def remote(source, target, send, recv, where):
        return pltpu.make_async_remote_copy(
            src_ref=source,
            dst_ref=target,
            send_sem=send,
            recv_sem=recv,
            device_id=where,
            device_id_type=pl.DeviceIdType.MESH,
        )

    def around(turn):
        return (col + turn) % inner

    def side(turn):
        return [
            remote(
                source,
                target.at[base + col],
                side_send.at[flow, turn - 1],
                side_recv.at[flow, turn - 1],
                (seq, around(turn)),
            )
            for flow, (source, target) in enumerate(firsts)
        ]

    def side_arrival(turn):
        return [
            remote(
                source,
                target.at[base + around(turn)],
                side_send.at[flow, inner - turn - 1],
                side_recv.at[flow, inner - turn - 1],
                (seq, around(turn)),
            )
            for flow, (source, target) in enumerate(firsts)
        ]

    def fore(hop, turn):
        return [
            remote(
                source if turn == 0 else target.at[base + around(turn)],
                target.at[(shards - hop) * inner + around(turn)],
                fore_send.at[flow, hop - 1, turn],
                fore_recv.at[flow, hop - 1, turn],
                (seq + hop, col),
            )
            for flow, (source, target) in enumerate(firsts)
        ]

    def near(step):
        there = me + step
        return [
            remote(
                source,
                target.at[reach[1] - step],
                near_send.at[flow, step - 1],
                near_recv.at[flow, step - 1],
                (there // inner, there % inner),
            )
            for flow, (source, target) in enumerate(seconds)
        ]

    def wanted(hop, turn):
        return hop * inner <= reach[0] + around(turn) - col

    def greet(where):
        pl.semaphore_signal(barrier, inc=1, device_id=where, device_id_type=pl.DeviceIdType.MESH)

    barrier = pltpu.get_barrier_semaphore()
    hops = (reach[0] + inner - 1 - col) // inner
    for turn in range(1, inner):
        greet((seq, around(turn)))
    for hop in range(1, shards + 1):

        @pl.when((seq - hop >= 0) & (hop <= hops))
        def _():
            greet((seq - hop, col))

    for step in range(1, reach[1] + 1):

        @pl.when(me - step >= 0)
        def _():
            greet(((me - step) // inner, (me - step) % inner))

    peers = inner - 1 + jnp.minimum(hops, outer - 1 - seq) + jnp.minimum(reach[1], count - 1 - me)
    pl.semaphore_wait(barrier, peers)

    for turn in range(1, inner):
        for copy in side(turn):
            copy.start()
    for turn in range(inner):
        if turn:
            for copy in side_arrival(turn):
                copy.wait_recv()
        for hop in range(shards, 0, -1):

            @pl.when((seq + hop < outer) & wanted(hop, turn))
            def _():
                for copy in fore(hop, turn):
                    copy.start()

        if turn == 0:
            for step in range(1, reach[1] + 1):

                @pl.when(me + step < count)
                def _():
                    for copy in near(step):
                        copy.start()

    for turn in range(inner):
        for hop in range(shards, 0, -1):

            @pl.when((seq - hop >= 0) & wanted(hop, turn))
            def _():
                for copy in fore(hop, turn):
                    copy.wait_recv()

            @pl.when((seq + hop < outer) & wanted(hop, turn))
            def _():
                for copy in fore(hop, turn):
                    copy.wait_send()

    for step in range(1, reach[1] + 1):

        @pl.when(me - step >= 0)
        def _():
            for copy in near(step):
                copy.wait_recv()

        @pl.when(me + step < count)
        def _():
            for copy in near(step):
                copy.wait_send()

    for turn in range(1, inner):
        for copy in side(turn):
            copy.wait_send()


def attend_kernel(*refs):
    q_far, far, out, q, near, fetched = refs[0], refs[1:9], refs[9], refs[10], refs[11:19], refs[19]
    k1f, v1f, k2f, v2f, kw, vt, vold, vnew, spread2, num_ref, den_ref, raised, scores = refs[20:]
    piece, heads, depth = q.shape
    inner = lax.axis_size("head")
    reach = near[0].shape[0]
    skip = lax.axis_index("head") + shards_behind(reach, inner) * inner - reach
    far = [far[0].at[pl.ds(skip, reach)], far[1].at[pl.ds(skip, reach)], *far[2:]]
    fetches = [
        pltpu.make_async_copy(source, target, fetched.at[index])
        for index, (source, target) in enumerate(zip(far, near))
    ]
    early = pltpu.make_async_copy(q_far.at[pl.ds(0, 1)], q.at[pl.ds(0, 1)], fetched.at[8])
    rest = pltpu.make_async_copy(q_far.at[pl.ds(1, piece - 1)], q.at[pl.ds(1, piece - 1)], fetched.at[9])
    for fetch in fetches:
        fetch.start()
    early.start()
    rest.start()
    k1h, v1h, k2h, v2h, k1, v1, k2, v2 = near
    for fetch in fetches:
        fetch.wait()
    me = lax.axis_index("seq") * inner + lax.axis_index("head")
    lead_one = k1h.shape[0] * piece
    lead_two = k2h.shape[0] * piece
    scale = math.log2(math.e) / math.sqrt(depth)

    def spread(target, behind, own):
        for slot in range(behind.shape[0]):
            target[slot * piece : (slot + 1) * piece, :] = behind[slot].astype(jnp.float32)
        lead = behind.shape[0] * piece
        target[lead : lead + piece, :] = own[...].astype(jnp.float32)
        if lead + piece < target.shape[0]:
            target[lead + piece :, :] = jnp.zeros((target.shape[0] - lead - piece, depth), jnp.float32)

    spread(k1f, k1h, k1)
    spread(v1f, v1h, v1)
    spread(k2f, k2h, k2)
    spread(v2f, v2h, v2)
    first_one = lead_one - me * piece
    first_two = lead_two - me * piece

    @pl.when(first_one > 0)
    def _():
        pos = lax.broadcasted_iota(jnp.int32, k1f.shape, 0)
        whole = k1f[...]
        head_row = jnp.sum(jnp.where(pos == first_one, whole, 0.0), axis=0, keepdims=True)
        k1f[...] = jnp.where(pos < first_one, head_row, whole)
        v1f[...] = jnp.where(pos < first_one, 0.0, v1f[...])

    pos_two = lax.broadcasted_iota(jnp.int32, k2f.shape, 0)
    whole_two = k2f[...]
    head_two = jnp.sum(jnp.where(pos_two == first_two, whole_two, 0.0), axis=0, keepdims=True)
    k2f[...] = jnp.where(pos_two < first_two, head_two, whole_two) * scale
    pos_v = lax.broadcasted_iota(jnp.int32, v2f.shape, 0)
    v2f[...] = jnp.where(pos_v < first_two, 0.0, v2f[...])

    span = LAG_CHUNK * heads
    chunks = WIN_TWO // LAG_CHUNK
    start_one = lead_one - WIN_ONE
    fresh = -(-piece // 16) * 16
    lane = lax.broadcasted_iota(jnp.int32, (depth + 16, depth), 1)
    sub = lax.broadcasted_iota(jnp.int32, (depth + 16, depth), 0)
    row_f = lax.broadcasted_iota(jnp.int32, (fresh, depth), 0)

    kw[...] = k1f[start_one : start_one + WIN_ONE, :].astype(jnp.bfloat16)
    for lo in range(0, WIN_ONE, depth):
        turned = jnp.transpose(v1f[start_one + lo : start_one + lo + depth, :])
        valid = jnp.where(lane[depth:] + (start_one + lo) < first_one, 0.0, 1.0)
        made = jnp.concatenate([turned, valid], axis=0)
        if lo == 0:
            vold[...] = made
        else:
            vt[:, lo : lo + depth] = made.astype(jnp.bfloat16)
    vnew[...] = jnp.concatenate(
        [jnp.transpose(v1f[lead_one : lead_one + depth, :]), jnp.ones((16, depth), jnp.float32)], axis=0
    )

    def load_keys(token):
        head = jnp.where(row_f <= token, k1f[lead_one : lead_one + fresh, :], k1f[start_one : start_one + fresh, :])
        kw[:fresh, :] = head.astype(jnp.bfloat16)

    def load_values(token):
        vt[:, :depth] = jnp.where(lane <= token, vnew[...], vold[...]).astype(jnp.bfloat16)

    behind_two = WIN_TWO - 1

    def spread_values(index):
        row = lead_two - behind_two + index
        late = jnp.broadcast_to(v2f[pl.ds(row + 1, 1), :], (heads, depth))
        soon = jnp.broadcast_to(v2f[pl.ds(row, 1), :], (heads, depth))
        spread2[index] = jnp.transpose(jnp.concatenate([late, soon], axis=0))

    own = jnp.where(lane[:depth] == sub[:depth], 1.0, 0.0).astype(jnp.bfloat16)
    for index in range(0, behind_two - 1, 2):
        rows = []
        for at in (index, index + 1):
            row = lead_two - behind_two + at
            rows.append(jnp.broadcast_to(v2f[row + 1 : row + 2, :], (heads, depth)))
            rows.append(jnp.broadcast_to(v2f[row : row + 1, :], (heads, depth)))
        made = lax.dot_general(
            own,
            jnp.concatenate(rows, axis=0).astype(jnp.bfloat16),
            (((1,), (1,)), ((), ())),
            preferred_element_type=jnp.float32,
        )
        spread2[index] = made[:, :depth]
        spread2[index + 1] = made[:, depth:]

    def products(token, chunk):
        query = q[token].astype(jnp.float32)
        rows = []
        for lag in range(chunk * LAG_CHUNK, (chunk + 1) * LAG_CHUNK):
            near = k2f[pl.ds(lead_two + token - lag, 1), :]
            rows.append((query * near).astype(jnp.bfloat16))
        return jnp.concatenate(rows, axis=0)

    def logits(token, chunk, top):
        product = products(token, chunk)
        for lo in range(0, WIN_ONE, WIN_ONE // ROW_L):
            made = lax.dot_general(
                kw[lo : lo + WIN_ONE // ROW_L, :],
                product,
                (((1,), (1,)), ((), ())),
                preferred_element_type=jnp.float32,
            )
            scores[lo : lo + WIN_ONE // ROW_L, chunk * span : (chunk + 1) * span] = made
            best = jnp.max(made.reshape(WIN_ONE // ROW_L // 8, 8, span), axis=0)
            parts = [best[:, at : at + depth] for at in range(0, span, depth)]
            top = parts if top is None else [jnp.maximum(a, b) for a, b in zip(top, parts)]
        return top

    num_ref[...] = jnp.zeros(num_ref.shape, jnp.float32)
    den_ref[...] = jnp.ones(den_ref.shape, jnp.float32)

    def finish(token, num, den):
        den = den + pltpu.roll(den, heads, 1)
        inverse = 1.0 / den
        num = num.reshape(depth // 8, 8, depth) * inverse[None]
        turned = jnp.transpose(num.reshape(depth, depth))
        out[token] = (turned[:heads] + turned[heads:]).astype(out.dtype)

    def weigh(chunk, peak):
        parts = scores[:, chunk * span : (chunk + 1) * span].reshape(WIN_ONE // 8, 8, span)
        raised[chunk] = jnp.exp2(parts - peak[None]).astype(jnp.bfloat16).reshape(WIN_ONE, span)

    def blend(token, chunk, num, den):
        mixed = jnp.dot(vt[...], raised[chunk], preferred_element_type=jnp.float32)
        for at in range(0, span, depth):
            lag = chunk * LAG_CHUNK + at // heads
            more = mixed[:depth, at : at + depth] * spread2[token - lag + behind_two - 1]
            known = jnp.where(lane[:8] // heads + (lag - token) <= me * piece, 1.0, 0.0)
            count = mixed[depth : depth + 8, at : at + depth] * known
            num = more if num is None else num + more
            den = count if den is None else den + count
        return num, den

    def last_blend(token):
        num, den = blend(token, chunks - 1, num_ref[...], den_ref[...])
        finish(token, num, den)

    def step(token, top):
        later = jnp.minimum(token + 1, piece - 1)
        peak = jnp.max(functools.reduce(jnp.maximum, top), axis=0, keepdims=True)
        peak = jnp.broadcast_to(jnp.maximum(peak, pltpu.roll(peak, heads, 1)), (8, depth))
        peak = jnp.concatenate([peak] * (span // depth), axis=1)
        last_blend(jnp.maximum(token - 1, 0))
        load_values(token)
        load_keys(later)
        spread_values(token + behind_two - 1)
        num = den = later_top = None
        for chunk in range(chunks):
            if chunk:
                num, den = blend(token, chunk - 1, num, den)
            weigh(chunk, peak)
            later_top = logits(later, chunk, later_top)
        num_ref[...] = num
        den_ref[...] = den
        return later_top

    def plain(token, chunk):
        raised[chunk] = jnp.exp2(
            lax.dot_general(
                kw[...], products(token, chunk), (((1,), (1,)), ((), ())), preferred_element_type=jnp.float32
            )
        ).astype(jnp.bfloat16)

    def quick(token, carry):
        last_blend(jnp.maximum(token - 1, 0))
        load_values(token)
        load_keys(token)
        spread_values(token + behind_two - 1)
        num = den = None
        for chunk in range(chunks):
            plain(token, chunk)
            if chunk:
                num, den = blend(token, chunk - 1, num, den)
        num_ref[...] = num
        den_ref[...] = den
        return carry

    def limit_squared():
        most = jnp.max(jnp.abs(q[...].astype(jnp.float32)), axis=1)
        most = (most * most).astype(jnp.bfloat16)
        twos = k2f[...]
        twos = (twos * twos).astype(jnp.bfloat16)
        ones = k1f[...]
        ones = (ones * ones).astype(jnp.bfloat16)
        over = (((1,), (1,)), ((), ()))
        left = lax.dot_general(most, twos, over, preferred_element_type=jnp.float32)
        right = lax.dot_general(
            ones, jnp.ones((depth, depth), jnp.bfloat16), over, preferred_element_type=jnp.float32
        )
        return 1.05 * jnp.max(left) * jnp.max(right)

    def shifted():
        load_keys(0)
        top = None
        for chunk in range(chunks):
            top = logits(0, chunk, top)
        lax.fori_loop(0, piece, step, top)

    def plainly():
        lax.fori_loop(0, piece, quick, 0, unroll=math.gcd(piece, UNROLL))

    early.wait()
    rest.wait()
    small = limit_squared() < SAFE * SAFE

    @pl.when(small)
    def _():
        plainly()

    @pl.when(jnp.logical_not(small))
    def _():
        shifted()

    last_blend(piece - 1)


def body(queries, key_one, value_one, key_two, value_two):
    piece, heads, depth = queries.shape
    reach = (pieces_behind(WIN_ONE, piece), pieces_behind(WIN_TWO, piece))
    anywhere = pl.BlockSpec(memory_space=pl.ANY)
    vmem = pl.BlockSpec(memory_space=pltpu.VMEM)
    inner = lax.axis_size("head")
    shards = shards_behind(reach[0], inner)
    slots = (shards + 1) * inner
    behind = [jax.ShapeDtypeStruct((r, piece, depth), key_one.dtype) for r in (slots, slots, reach[1], reach[1])]
    windows = [jax.ShapeDtypeStruct((r, piece, depth), key_one.dtype) for r in (reach[0], reach[0], reach[1], reach[1])]
    halos = pl.pallas_call(
        functools.partial(halo_kernel, reach),
        out_shape=behind,
        in_specs=[anywhere] * 4,
        out_specs=[anywhere] * 4,
        scratch_shapes=[
            *[pltpu.SemaphoreType.DMA((2, inner))] * 2,
            *[pltpu.SemaphoreType.DMA((2, shards, inner))] * 2,
            *[pltpu.SemaphoreType.DMA((2, reach[1]))] * 2,
        ],
        compiler_params=pltpu.CompilerParams(collective_id=0, has_side_effects=True),
    )(key_one, value_one, key_two, value_two)
    long_one = (reach[0] * piece + depth, depth)
    long_two = (reach[1] * piece + depth, depth)
    return pl.pallas_call(
        attend_kernel,
        out_shape=jax.ShapeDtypeStruct(queries.shape, queries.dtype),
        in_specs=[anywhere] * 9,
        out_specs=vmem,
        scratch_shapes=[
            pltpu.VMEM(queries.shape, queries.dtype),
            *[pltpu.VMEM(x.shape, x.dtype) for x in (*windows, key_one, value_one, key_two, value_two)],
            pltpu.SemaphoreType.DMA((10,)),
            pltpu.VMEM(long_one, jnp.float32),
            pltpu.VMEM(long_one, jnp.float32),
            pltpu.VMEM(long_two, jnp.float32),
            pltpu.VMEM(long_two, jnp.float32),
            pltpu.VMEM((WIN_ONE, depth), jnp.bfloat16),
            pltpu.VMEM((depth + 16, WIN_ONE), jnp.bfloat16),
            pltpu.VMEM((depth + 16, depth), jnp.float32),
            pltpu.VMEM((depth + 16, depth), jnp.float32),
            pltpu.VMEM((piece + WIN_TWO - 2, depth, depth), jnp.float32),
            pltpu.VMEM((depth, depth), jnp.float32),
            pltpu.VMEM((8, depth), jnp.float32),
            pltpu.VMEM((WIN_TWO // LAG_CHUNK, WIN_ONE, LAG_CHUNK * heads), jnp.bfloat16),
            pltpu.VMEM((WIN_ONE, WIN_TWO * heads), jnp.float32),
        ],
    )(queries, *halos, key_one, value_one, key_two, value_two)


def solution(mesh):
    rows = P(("seq", "head"), None)
    placed = (P(("seq", "head"), None, None), rows, rows, rows, rows)
    return jax.shard_map(
        body, mesh=mesh, in_specs=placed, out_specs=P(("seq", "head"), None, None), check_vma=False
    )
```

```python
import functools
import math

import jax
import jax.numpy as jnp
from jax import lax
from jax.experimental import pallas as pl
from jax.experimental.pallas import tpu as pltpu
from jax.sharding import PartitionSpec as P

WIN_ONE = 512
WIN_TWO = 32
LAG_CHUNK = 8
ROW_L = 1
SAFE = 100.0
HALO_VMEM = 8 << 20
ATTEND_VMEM = 24 << 20
UNROLL = 8


def pieces_behind(window, rows):
    return (window - 1) // rows + 1


def shards_behind(reach, inner):
    return (reach + inner - 1) // inner


def halo_kernel(reach, q, k1, v1, k2, v2, k1_out, v1_out, k2_out, v2_out, q_out, spread2, most, *rest):
    side_send, side_recv, fore_send, fore_recv, near_send, near_recv, local, v2f = rest
    inner, outer = lax.axis_size("head"), lax.axis_size("seq")
    seq, col = lax.axis_index("seq"), lax.axis_index("head")
    me, count = seq * inner + col, outer * inner
    shards = shards_behind(reach[0], inner)
    base = shards * inner
    firsts = ((k1, k1_out), (v1, v1_out))
    seconds = ((k2, k2_out), (v2, v2_out))

    def remote(source, target, send, recv, where):
        return pltpu.make_async_remote_copy(
            src_ref=source,
            dst_ref=target,
            send_sem=send,
            recv_sem=recv,
            device_id=where,
            device_id_type=pl.DeviceIdType.MESH,
        )

    def around(turn):
        other, bit = col, 1
        while bit < inner:
            if turn & bit:
                other = other + bit - 2 * bit * ((col // bit) % 2)
            bit = 2 * bit
        return other

    def side(turn):
        return [
            remote(
                target.at[base + col],
                target.at[base + col],
                side_send.at[flow, turn - 1],
                side_recv.at[flow, turn - 1],
                (seq, around(turn)),
            )
            for flow, (source, target) in enumerate(firsts)
        ]

    def side_arrival(turn):
        return [
            remote(
                target.at[base + around(turn)],
                target.at[base + around(turn)],
                side_send.at[flow, turn - 1],
                side_recv.at[flow, turn - 1],
                (seq, around(turn)),
            )
            for flow, (source, target) in enumerate(firsts)
        ]

    def fore(hop, turn):
        return [
            remote(
                target.at[base + around(turn)],
                target.at[(shards - hop) * inner + around(turn)],
                fore_send.at[flow, hop - 1, turn],
                fore_recv.at[flow, hop - 1, turn],
                (seq + hop, col),
            )
            for flow, (source, target) in enumerate(firsts)
        ]

    def near(step):
        there = me + step
        return [
            remote(
                target.at[reach[1]],
                target.at[reach[1] - step],
                near_send.at[flow, step - 1],
                near_recv.at[flow, step - 1],
                (there // inner, there % inner),
            )
            for flow, (source, target) in enumerate(seconds)
        ]

    def wanted(hop, turn):
        return hop * inner <= reach[0] + around(turn) - col

    def greet(where):
        pl.semaphore_signal(barrier, inc=1, device_id=where, device_id_type=pl.DeviceIdType.MESH)

    places = [base + col, base + col, reach[1], reach[1]]
    fetches = [
        pltpu.make_async_copy(source, target.at[place], local.at[index])
        for index, ((source, target), place) in enumerate(zip(firsts + seconds, places))
    ]
    fetches.append(pltpu.make_async_copy(q, q_out, local.at[4]))
    for fetch in fetches:
        fetch.start()
    barrier = pltpu.get_barrier_semaphore()
    hops = (reach[0] + inner - 1 - col) // inner
    for turn in range(1, inner):
        greet((seq, around(turn)))
    for hop in range(1, shards + 1):

        @pl.when((seq - hop >= 0) & (hop <= hops))
        def _():
            greet((seq - hop, col))

    for step in range(1, reach[1] + 1):

        @pl.when(me - step >= 0)
        def _():
            greet(((me - step) // inner, (me - step) % inner))

    peers = inner - 1 + jnp.minimum(hops, outer - 1 - seq) + jnp.minimum(reach[1], count - 1 - me)
    pl.semaphore_wait(barrier, peers)
    for fetch in fetches[:4]:
        fetch.wait()

    for turn in range(1, inner):
        for copy in side(turn):
            copy.start()
    for turn in range(inner):
        if turn:
            for copy in side_arrival(turn):
                copy.wait_recv()
        for hop in range(shards, 0, -1):

            @pl.when((seq + hop < outer) & wanted(hop, turn))
            def _():
                for copy in fore(hop, turn):
                    copy.start()

        if turn == 0:
            for step in range(1, reach[1] + 1):

                @pl.when(me + step < count)
                def _():
                    for copy in near(step):
                        copy.start()

    for step in range(1, reach[1] + 1):

        @pl.when(me - step >= 0)
        def _():
            for copy in near(step):
                copy.wait_recv()

    spread_tables(reach, me, v2_out, v2f, spread2, q_out.shape[1])
    fetches[4].wait()
    most[...] = jnp.max(jnp.abs(q_out[...].astype(jnp.float32)), axis=1)

    for turn in range(inner):
        for hop in range(shards, 0, -1):

            @pl.when((seq - hop >= 0) & wanted(hop, turn))
            def _():
                for copy in fore(hop, turn):
                    copy.wait_recv()

            @pl.when((seq + hop < outer) & wanted(hop, turn))
            def _():
                for copy in fore(hop, turn):
                    copy.wait_send()

    for step in range(1, reach[1] + 1):

        @pl.when(me + step < count)
        def _():
            for copy in near(step):
                copy.wait_send()

    for turn in range(1, inner):
        for copy in side(turn):
            copy.wait_send()


def spread_tables(reach, me, v2, v2f, spread2, heads):
    slots, piece, depth = v2.shape
    lead_two = reach[1] * piece
    for slot in range(slots):
        v2f[slot * piece : (slot + 1) * piece, :] = v2[slot].astype(jnp.float32)
    pos = lax.broadcasted_iota(jnp.int32, v2f.shape, 0)
    v2f[...] = jnp.where(pos < lead_two - me * piece, 0.0, v2f[...])
    lane = lax.broadcasted_iota(jnp.int32, (depth, depth), 1)
    sub = lax.broadcasted_iota(jnp.int32, (depth, depth), 0)
    own = jnp.where(lane == sub, 1.0, 0.0).astype(jnp.bfloat16)
    for index in range(0, spread2.shape[0], 2):
        rows = []
        for at in range(index, min(index + 2, spread2.shape[0])):
            row = lead_two - (WIN_TWO - 1) + at
            rows.append(jnp.broadcast_to(v2f[row + 1 : row + 2, :], (heads, depth)))
            rows.append(jnp.broadcast_to(v2f[row : row + 1, :], (heads, depth)))
        made = lax.dot_general(
            own,
            jnp.concatenate(rows, axis=0).astype(jnp.bfloat16),
            (((1,), (1,)), ((), ())),
            preferred_element_type=jnp.float32,
        )
        spread2[index] = made[:, :depth]
        if index + 1 < spread2.shape[0]:
            spread2[index + 1] = made[:, depth:]


def attend_kernel(*refs):
    k1h, v1h, k2h, v2h, q, spread2, most_ref, out = refs[:8]
    k1f, v1f, k2f, kw, vt, vold, vnew, num_ref, den_ref, raised, scores = refs[8:]
    piece, heads, depth = q.shape
    inner = lax.axis_size("head")
    reach = pieces_behind(WIN_ONE, piece)
    skip = lax.axis_index("head") + shards_behind(reach, inner) * inner - reach
    me = lax.axis_index("seq") * inner + lax.axis_index("head")
    lead_one = reach * piece
    lead_two = (k2h.shape[0] - 1) * piece
    scale = math.log2(math.e) / math.sqrt(depth)

    def spread(target, behind, skip, count):
        for slot in range(count):
            target[slot * piece : (slot + 1) * piece, :] = behind[skip + slot].astype(jnp.float32)
        if count * piece < target.shape[0]:
            target[count * piece :, :] = jnp.zeros((target.shape[0] - count * piece, depth), jnp.float32)

    spread(k1f, k1h, skip, reach + 1)
    spread(v1f, v1h, skip, reach + 1)
    spread(k2f, k2h, 0, k2h.shape[0])
    first_one = lead_one - me * piece
    first_two = lead_two - me * piece

    @pl.when(first_one > 0)
    def _():
        pos = lax.broadcasted_iota(jnp.int32, k1f.shape, 0)
        whole = k1f[...]
        head_row = jnp.sum(jnp.where(pos == first_one, whole, 0.0), axis=0, keepdims=True)
        k1f[...] = jnp.where(pos < first_one, head_row, whole)
        v1f[...] = jnp.where(pos < first_one, 0.0, v1f[...])

    pos_two = lax.broadcasted_iota(jnp.int32, k2f.shape, 0)
    whole_two = k2f[...]
    head_two = jnp.sum(jnp.where(pos_two == first_two, whole_two, 0.0), axis=0, keepdims=True)
    k2f[...] = jnp.where(pos_two < first_two, head_two, whole_two) * scale

    span = LAG_CHUNK * heads
    chunks = WIN_TWO // LAG_CHUNK
    start_one = lead_one - WIN_ONE
    fresh = -(-piece // 16) * 16
    lane = lax.broadcasted_iota(jnp.int32, (depth + 16, depth), 1)
    sub = lax.broadcasted_iota(jnp.int32, (depth + 16, depth), 0)
    row_f = lax.broadcasted_iota(jnp.int32, (fresh, depth), 0)

    kw[...] = k1f[start_one : start_one + WIN_ONE, :].astype(jnp.bfloat16)
    for lo in range(0, WIN_ONE, depth):
        turned = jnp.transpose(v1f[start_one + lo : start_one + lo + depth, :])
        valid = jnp.where(lane[depth:] + (start_one + lo) < first_one, 0.0, 1.0)
        made = jnp.concatenate([turned, valid], axis=0)
        if lo == 0:
            vold[...] = made
        else:
            vt[:, lo : lo + depth] = made.astype(jnp.bfloat16)
    vnew[...] = jnp.concatenate(
        [jnp.transpose(v1f[lead_one : lead_one + depth, :]), jnp.ones((16, depth), jnp.float32)], axis=0
    )

    def load_keys(token):
        head = jnp.where(row_f <= token, k1f[lead_one : lead_one + fresh, :], k1f[start_one : start_one + fresh, :])
        kw[:fresh, :] = head.astype(jnp.bfloat16)

    def load_values(token):
        vt[:, :depth] = jnp.where(lane <= token, vnew[...], vold[...]).astype(jnp.bfloat16)

    behind_two = WIN_TWO - 1

    def products(token, chunk):
        query = q[token].astype(jnp.float32)
        rows = []
        for lag in range(chunk * LAG_CHUNK, (chunk + 1) * LAG_CHUNK):
            near = k2f[pl.ds(lead_two + token - lag, 1), :]
            rows.append((query * near).astype(jnp.bfloat16))
        return jnp.concatenate(rows, axis=0)

    def logits(token, chunk, top):
        product = products(token, chunk)
        for lo in range(0, WIN_ONE, WIN_ONE // ROW_L):
            made = lax.dot_general(
                kw[lo : lo + WIN_ONE // ROW_L, :],
                product,
                (((1,), (1,)), ((), ())),
                preferred_element_type=jnp.float32,
            )
            scores[lo : lo + WIN_ONE // ROW_L, chunk * span : (chunk + 1) * span] = made
            best = jnp.max(made.reshape(WIN_ONE // ROW_L // 8, 8, span), axis=0)
            parts = [best[:, at : at + depth] for at in range(0, span, depth)]
            top = parts if top is None else [jnp.maximum(a, b) for a, b in zip(top, parts)]
        return top

    num_ref[...] = jnp.zeros(num_ref.shape, jnp.float32)
    den_ref[...] = jnp.ones(den_ref.shape, jnp.float32)

    def finish(token, num, den):
        den = den + pltpu.roll(den, heads, 1)
        inverse = 1.0 / den
        num = num.reshape(depth // 8, 8, depth) * inverse[None]
        turned = jnp.transpose(num.reshape(depth, depth))
        out[token] = (turned[:heads] + turned[heads:]).astype(out.dtype)

    def weigh(chunk, peak):
        parts = scores[:, chunk * span : (chunk + 1) * span].reshape(WIN_ONE // 8, 8, span)
        raised[chunk] = jnp.exp2(parts - peak[None]).astype(jnp.bfloat16).reshape(WIN_ONE, span)

    def blend(token, chunk, num, den):
        mixed = jnp.dot(vt[...], raised[chunk], preferred_element_type=jnp.float32)
        for at in range(0, span, depth):
            lag = chunk * LAG_CHUNK + at // heads
            more = mixed[:depth, at : at + depth] * spread2[token - lag + behind_two - 1]
            known = jnp.where(lane[:8] // heads + (lag - token) <= me * piece, 1.0, 0.0)
            count = mixed[depth : depth + 8, at : at + depth] * known
            num = more if num is None else num + more
            den = count if den is None else den + count
        return num, den

    def last_blend(token):
        num, den = blend(token, chunks - 1, num_ref[...], den_ref[...])
        finish(token, num, den)

    def step(token, top):
        later = jnp.minimum(token + 1, piece - 1)
        peak = jnp.max(functools.reduce(jnp.maximum, top), axis=0, keepdims=True)
        peak = jnp.broadcast_to(jnp.maximum(peak, pltpu.roll(peak, heads, 1)), (8, depth))
        peak = jnp.concatenate([peak] * (span // depth), axis=1)
        last_blend(jnp.maximum(token - 1, 0))
        load_values(token)
        load_keys(later)
        num = den = later_top = None
        for chunk in range(chunks):
            if chunk:
                num, den = blend(token, chunk - 1, num, den)
            weigh(chunk, peak)
            later_top = logits(later, chunk, later_top)
        num_ref[...] = num
        den_ref[...] = den
        return later_top

    def plain(token, chunk):
        raised[chunk] = jnp.exp2(
            lax.dot_general(
                kw[...], products(token, chunk), (((1,), (1,)), ((), ())), preferred_element_type=jnp.float32
            )
        ).astype(jnp.bfloat16)

    def quick(token, carry):
        last_blend(jnp.maximum(token - 1, 0))
        load_values(token)
        load_keys(token)
        num = den = None
        for chunk in range(chunks):
            plain(token, chunk)
            if chunk:
                num, den = blend(token, chunk - 1, num, den)
        num_ref[...] = num
        den_ref[...] = den
        return carry

    def limit_squared():
        most = most_ref[...]
        most = (most * most).astype(jnp.bfloat16)
        twos = k2f[...]
        twos = (twos * twos).astype(jnp.bfloat16)
        ones = k1f[...]
        ones = (ones * ones).astype(jnp.bfloat16)
        over = (((1,), (1,)), ((), ()))
        left = lax.dot_general(most, twos, over, preferred_element_type=jnp.float32)
        right = lax.dot_general(
            ones, jnp.ones((depth, depth), jnp.bfloat16), over, preferred_element_type=jnp.float32
        )
        return 1.05 * jnp.max(left) * jnp.max(right)

    def shifted():
        load_keys(0)
        top = None
        for chunk in range(chunks):
            top = logits(0, chunk, top)
        lax.fori_loop(0, piece, step, top)

    def plainly():
        lax.fori_loop(0, piece, quick, 0, unroll=math.gcd(piece, UNROLL))

    small = limit_squared() < SAFE * SAFE

    @pl.when(small)
    def _():
        plainly()

    @pl.when(jnp.logical_not(small))
    def _():
        shifted()

    last_blend(piece - 1)


def body(queries, key_one, value_one, key_two, value_two):
    piece, heads, depth = queries.shape
    reach = (pieces_behind(WIN_ONE, piece), pieces_behind(WIN_TWO, piece))
    vmem = pl.BlockSpec(memory_space=pltpu.VMEM)
    inner = lax.axis_size("head")
    shards = shards_behind(reach[0], inner)
    slots = ((shards + 1) * inner, (shards + 1) * inner, reach[1] + 1, reach[1] + 1)
    long_one = (reach[0] * piece + depth, depth)
    long_two = (reach[1] * piece + depth, depth)
    made = pl.pallas_call(
        functools.partial(halo_kernel, reach),
        out_shape=[
            *[pltpu.VMEM((slot, piece, depth), key_one.dtype) for slot in slots],
            pltpu.VMEM(queries.shape, queries.dtype),
            pltpu.VMEM((piece + WIN_TWO - 2, depth, depth), jnp.float32),
            pltpu.VMEM((piece, depth), jnp.float32),
        ],
        in_specs=[pl.BlockSpec(memory_space=pltpu.HBM)] * 5,
        out_specs=[vmem] * 7,
        scratch_shapes=[
            *[pltpu.SemaphoreType.DMA((2, inner))] * 2,
            *[pltpu.SemaphoreType.DMA((2, shards, inner))] * 2,
            *[pltpu.SemaphoreType.DMA((2, reach[1]))] * 2,
            pltpu.SemaphoreType.DMA((5,)),
            pltpu.VMEM(((reach[1] + 1) * piece, depth), jnp.float32),
        ],
        compiler_params=pltpu.CompilerParams(
            collective_id=0, has_side_effects=True, vmem_limit_bytes=HALO_VMEM
        ),
    )(*[pltpu.with_memory_space_constraint(x, pltpu.HBM) for x in (queries, key_one, value_one, key_two, value_two)])
    made = [
        pltpu.with_memory_space_constraint(made[index], pltpu.VMEM) for index in (0, 1, 2, 3, 4, 5, 6)
    ]
    return pl.pallas_call(
        attend_kernel,
        out_shape=jax.ShapeDtypeStruct(queries.shape, queries.dtype),
        in_specs=[vmem] * 7,
        out_specs=vmem,
        scratch_shapes=[
            pltpu.VMEM(long_one, jnp.float32),
            pltpu.VMEM(long_one, jnp.float32),
            pltpu.VMEM(long_two, jnp.float32),
            pltpu.VMEM((WIN_ONE, depth), jnp.bfloat16),
            pltpu.VMEM((depth + 16, WIN_ONE), jnp.bfloat16),
            pltpu.VMEM((depth + 16, depth), jnp.float32),
            pltpu.VMEM((depth + 16, depth), jnp.float32),
            pltpu.VMEM((depth, depth), jnp.float32),
            pltpu.VMEM((8, depth), jnp.float32),
            pltpu.VMEM((WIN_TWO // LAG_CHUNK, WIN_ONE, LAG_CHUNK * heads), jnp.bfloat16),
            pltpu.VMEM((WIN_ONE, WIN_TWO * heads), jnp.float32),
        ],
        compiler_params=pltpu.CompilerParams(vmem_limit_bytes=ATTEND_VMEM),
    )(*made)


def solution(mesh):
    rows = P(("seq", "head"), None)
    placed = (P(("seq", "head"), None, None), rows, rows, rows, rows)
    return jax.shard_map(
        body, mesh=mesh, in_specs=placed, out_specs=P(("seq", "head"), None, None), check_vma=False
    )
```

```python
import functools
import math

import jax
import jax.numpy as jnp
from jax import lax
from jax.experimental import pallas as pl
from jax.experimental.pallas import tpu as pltpu
from jax.sharding import PartitionSpec as P

WIN_ONE = 512
WIN_TWO = 32
LAG_CHUNK = 8
ROW_L = 1
SAFE = 69.0
HALO_VMEM = 8 << 20
ATTEND_VMEM = 24 << 20
UNROLL = 20


def pieces_behind(window, rows):
    return (window - 1) // rows + 1


def shards_behind(reach, inner):
    return (reach + inner - 1) // inner


def halo_kernel(reach, q, k1, v1, k2, v2, k1_out, v1_out, k2_out, v2_out, q_out, spread2, most, *rest):
    side_send, side_recv, fore_send, fore_recv, near_send, near_recv, local, v2f = rest
    inner, outer = lax.axis_size("head"), lax.axis_size("seq")
    seq, col = lax.axis_index("seq"), lax.axis_index("head")
    me, count = seq * inner + col, outer * inner
    shards = shards_behind(reach[0], inner)
    base = shards * inner
    firsts = ((k1, k1_out), (v1, v1_out))
    seconds = ((k2, k2_out), (v2, v2_out))

    def remote(source, target, send, recv, where):
        return pltpu.make_async_remote_copy(
            src_ref=source,
            dst_ref=target,
            send_sem=send,
            recv_sem=recv,
            device_id=where,
            device_id_type=pl.DeviceIdType.MESH,
        )

    def around(turn):
        other, bit = col, 1
        while bit < inner:
            if turn & bit:
                other = other + bit - 2 * bit * ((col // bit) % 2)
            bit = 2 * bit
        return other

    def side(turn):
        return [
            remote(
                target.at[base + col],
                target.at[base + col],
                side_send.at[flow, turn - 1],
                side_recv.at[flow, turn - 1],
                (seq, around(turn)),
            )
            for flow, (source, target) in enumerate(firsts)
        ]

    def side_arrival(turn):
        return [
            remote(
                target.at[base + around(turn)],
                target.at[base + around(turn)],
                side_send.at[flow, turn - 1],
                side_recv.at[flow, turn - 1],
                (seq, around(turn)),
            )
            for flow, (source, target) in enumerate(firsts)
        ]

    def fore(hop, turn):
        return [
            remote(
                target.at[base + around(turn)],
                target.at[(shards - hop) * inner + around(turn)],
                fore_send.at[flow, hop - 1, turn],
                fore_recv.at[flow, hop - 1, turn],
                (seq + hop, col),
            )
            for flow, (source, target) in enumerate(firsts)
        ]

    def near(step):
        there = me + step
        return [
            remote(
                target.at[reach[1]],
                target.at[reach[1] - step],
                near_send.at[flow, step - 1],
                near_recv.at[flow, step - 1],
                (there // inner, there % inner),
            )
            for flow, (source, target) in enumerate(seconds)
        ]

    def wanted(hop, turn):
        return hop * inner <= reach[0] + around(turn) - col

    def greet(where):
        pl.semaphore_signal(barrier, inc=1, device_id=where, device_id_type=pl.DeviceIdType.MESH)

    places = [base + col, base + col, reach[1], reach[1]]
    fetches = [
        pltpu.make_async_copy(source, target.at[place], local.at[index])
        for index, ((source, target), place) in enumerate(zip(firsts + seconds, places))
    ]
    fetches.append(pltpu.make_async_copy(q, q_out, local.at[4]))
    for fetch in fetches:
        fetch.start()
    barrier = pltpu.get_barrier_semaphore()
    hops = (reach[0] + inner - 1 - col) // inner
    for turn in range(1, inner):
        greet((seq, around(turn)))
    for hop in range(1, shards + 1):

        @pl.when((seq - hop >= 0) & (hop <= hops))
        def _():
            greet((seq - hop, col))

    for step in range(1, reach[1] + 1):

        @pl.when(me - step >= 0)
        def _():
            greet(((me - step) // inner, (me - step) % inner))

    peers = inner - 1 + jnp.minimum(hops, outer - 1 - seq) + jnp.minimum(reach[1], count - 1 - me)
    pl.semaphore_wait(barrier, peers)
    for fetch in fetches[:4]:
        fetch.wait()

    for turn in range(1, inner):
        for copy in side(turn):
            copy.start()
    for turn in range(inner):
        if turn:
            for copy in side_arrival(turn):
                copy.wait_recv()
        for hop in range(shards, 0, -1):

            @pl.when((seq + hop < outer) & wanted(hop, turn))
            def _():
                for copy in fore(hop, turn):
                    copy.start()

        if turn == 0:
            for step in range(1, reach[1] + 1):

                @pl.when(me + step < count)
                def _():
                    for copy in near(step):
                        copy.start()

    for step in range(1, reach[1] + 1):

        @pl.when(me - step >= 0)
        def _():
            for copy in near(step):
                copy.wait_recv()

    spread_tables(reach, me, v2_out, v2f, spread2, q_out.shape[1])
    fetches[4].wait()
    most[...] = jnp.max(jnp.abs(q_out[...].astype(jnp.float32)), axis=1)

    for turn in range(inner):
        for hop in range(shards, 0, -1):

            @pl.when((seq - hop >= 0) & wanted(hop, turn))
            def _():
                for copy in fore(hop, turn):
                    copy.wait_recv()

            @pl.when((seq + hop < outer) & wanted(hop, turn))
            def _():
                for copy in fore(hop, turn):
                    copy.wait_send()

    for step in range(1, reach[1] + 1):

        @pl.when(me + step < count)
        def _():
            for copy in near(step):
                copy.wait_send()

    for turn in range(1, inner):
        for copy in side(turn):
            copy.wait_send()


def spread_tables(reach, me, v2, v2f, spread2, heads):
    slots, piece, depth = v2.shape
    lead_two = reach[1] * piece
    for slot in range(slots):
        v2f[slot * piece : (slot + 1) * piece, :] = v2[slot].astype(jnp.float32)
    pos = lax.broadcasted_iota(jnp.int32, v2f.shape, 0)
    v2f[...] = jnp.where(pos < lead_two - me * piece, 0.0, v2f[...])
    lane = lax.broadcasted_iota(jnp.int32, (depth, depth), 1)
    sub = lax.broadcasted_iota(jnp.int32, (depth, depth), 0)
    own = jnp.where(lane == sub, 1.0, 0.0).astype(jnp.bfloat16)
    for index in range(0, spread2.shape[0], 2):
        rows = []
        for at in range(index, min(index + 2, spread2.shape[0])):
            row = lead_two - (WIN_TWO - 1) + at
            rows.append(jnp.broadcast_to(v2f[row + 1 : row + 2, :], (heads, depth)))
            rows.append(jnp.broadcast_to(v2f[row : row + 1, :], (heads, depth)))
        made = lax.dot_general(
            own,
            jnp.concatenate(rows, axis=0).astype(jnp.bfloat16),
            (((1,), (1,)), ((), ())),
            preferred_element_type=jnp.float32,
        )
        spread2[index] = made[:, :depth]
        if index + 1 < spread2.shape[0]:
            spread2[index + 1] = made[:, depth:]


def attend_kernel(*refs):
    k1h, v1h, k2h, v2h, q, spread2, most_ref, out = refs[:8]
    k1f, v1f, k2f, kw, vt, vold, vnew, num_ref, den_ref, raised, scores = refs[8:]
    piece, heads, depth = q.shape
    inner = lax.axis_size("head")
    reach = pieces_behind(WIN_ONE, piece)
    skip = lax.axis_index("head") + shards_behind(reach, inner) * inner - reach
    me = lax.axis_index("seq") * inner + lax.axis_index("head")
    lead_one = reach * piece
    lead_two = (k2h.shape[0] - 1) * piece
    scale = 1.0 / math.sqrt(depth)

    def spread(target, behind, skip, count):
        for slot in range(count):
            target[slot * piece : (slot + 1) * piece, :] = behind[skip + slot].astype(jnp.float32)
        if count * piece < target.shape[0]:
            target[count * piece :, :] = jnp.zeros((target.shape[0] - count * piece, depth), jnp.float32)

    spread(k1f, k1h, skip, reach + 1)
    spread(v1f, v1h, skip, reach + 1)
    spread(k2f, k2h, 0, k2h.shape[0])
    first_one = lead_one - me * piece
    first_two = lead_two - me * piece

    @pl.when(first_one > 0)
    def _():
        pos = lax.broadcasted_iota(jnp.int32, k1f.shape, 0)
        whole = k1f[...]
        head_row = jnp.sum(jnp.where(pos == first_one, whole, 0.0), axis=0, keepdims=True)
        k1f[...] = jnp.where(pos < first_one, head_row, whole)
        v1f[...] = jnp.where(pos < first_one, 0.0, v1f[...])

    pos_two = lax.broadcasted_iota(jnp.int32, k2f.shape, 0)
    whole_two = k2f[...]
    head_two = jnp.sum(jnp.where(pos_two == first_two, whole_two, 0.0), axis=0, keepdims=True)
    k2f[...] = jnp.where(pos_two < first_two, head_two, whole_two) * scale

    span = LAG_CHUNK * heads
    chunks = WIN_TWO // LAG_CHUNK
    start_one = lead_one - WIN_ONE
    fresh = -(-piece // 16) * 16
    lane = lax.broadcasted_iota(jnp.int32, (depth + 16, depth), 1)
    sub = lax.broadcasted_iota(jnp.int32, (depth + 16, depth), 0)
    row_f = lax.broadcasted_iota(jnp.int32, (fresh, depth), 0)

    kw[...] = k1f[start_one : start_one + WIN_ONE, :].astype(jnp.bfloat16)
    for lo in range(0, WIN_ONE, depth):
        turned = jnp.transpose(v1f[start_one + lo : start_one + lo + depth, :])
        valid = jnp.where(lane[depth:] + (start_one + lo) < first_one, 0.0, 1.0)
        made = jnp.concatenate([turned, valid], axis=0)
        if lo == 0:
            vold[...] = made
        else:
            vt[:, lo : lo + depth] = made.astype(jnp.bfloat16)
    vnew[...] = jnp.concatenate(
        [jnp.transpose(v1f[lead_one : lead_one + depth, :]), jnp.ones((16, depth), jnp.float32)], axis=0
    )

    def load_keys(token):
        head = jnp.where(row_f <= token, k1f[lead_one : lead_one + fresh, :], k1f[start_one : start_one + fresh, :])
        kw[:fresh, :] = head.astype(jnp.bfloat16)

    def load_values(token):
        vt[:, :depth] = jnp.where(lane <= token, vnew[...], vold[...]).astype(jnp.bfloat16)

    behind_two = WIN_TWO - 1

    def products(token, chunk):
        query = q[token].astype(jnp.float32)
        rows = []
        for lag in range(chunk * LAG_CHUNK, (chunk + 1) * LAG_CHUNK):
            near = k2f[pl.ds(lead_two + token - lag, 1), :]
            rows.append((query * near).astype(jnp.bfloat16))
        return jnp.concatenate(rows, axis=0)

    def logits(token, chunk, top):
        product = products(token, chunk)
        for lo in range(0, WIN_ONE, WIN_ONE // ROW_L):
            made = lax.dot_general(
                kw[lo : lo + WIN_ONE // ROW_L, :],
                product,
                (((1,), (1,)), ((), ())),
                preferred_element_type=jnp.float32,
            )
            scores[lo : lo + WIN_ONE // ROW_L, chunk * span : (chunk + 1) * span] = made
            best = jnp.max(made.reshape(WIN_ONE // ROW_L // 8, 8, span), axis=0)
            parts = [best[:, at : at + depth] for at in range(0, span, depth)]
            top = parts if top is None else [jnp.maximum(a, b) for a, b in zip(top, parts)]
        return top

    num_ref[...] = jnp.zeros(num_ref.shape, jnp.float32)
    den_ref[...] = jnp.ones(den_ref.shape, jnp.float32)

    def finish(token, num, den):
        den = den + pltpu.roll(den, heads, 1)
        inverse = 1.0 / den
        num = num.reshape(depth // 8, 8, depth) * inverse[None]
        turned = jnp.transpose(num.reshape(depth, depth))
        out[token] = (turned[:heads] + turned[heads:]).astype(out.dtype)

    def weigh(chunk, peak):
        parts = scores[:, chunk * span : (chunk + 1) * span].reshape(WIN_ONE // 8, 8, span)
        raised[chunk] = jnp.exp(parts - peak[None]).astype(jnp.bfloat16).reshape(WIN_ONE, span)

    def blend(token, chunk, num, den):
        mixed = jnp.dot(vt[...], raised[chunk], preferred_element_type=jnp.float32)
        for at in range(0, span, depth):
            lag = chunk * LAG_CHUNK + at // heads
            more = mixed[:depth, at : at + depth] * spread2[token - lag + behind_two - 1]
            known = jnp.where(lane[:8] // heads + (lag - token) <= me * piece, 1.0, 0.0)
            count = mixed[depth : depth + 8, at : at + depth] * known
            num = more if num is None else num + more
            den = count if den is None else den + count
        return num, den

    def last_blend(token):
        num, den = blend(token, chunks - 1, num_ref[...], den_ref[...])
        finish(token, num, den)

    def step(token, top):
        later = jnp.minimum(token + 1, piece - 1)
        peak = jnp.max(functools.reduce(jnp.maximum, top), axis=0, keepdims=True)
        peak = jnp.broadcast_to(jnp.maximum(peak, pltpu.roll(peak, heads, 1)), (8, depth))
        peak = jnp.concatenate([peak] * (span // depth), axis=1)
        last_blend(jnp.maximum(token - 1, 0))
        load_values(token)
        load_keys(later)
        num = den = later_top = None
        for chunk in range(chunks):
            if chunk:
                num, den = blend(token, chunk - 1, num, den)
            weigh(chunk, peak)
            later_top = logits(later, chunk, later_top)
        num_ref[...] = num
        den_ref[...] = den
        return later_top

    def plain(token, chunk):
        raised[chunk] = jnp.exp(
            lax.dot_general(
                kw[...], products(token, chunk), (((1,), (1,)), ((), ())), preferred_element_type=jnp.float32
            )
        ).astype(jnp.bfloat16)

    def quick(token, carry):
        last_blend(jnp.maximum(token - 1, 0))
        load_values(token)
        load_keys(token)
        num = den = None
        for chunk in range(chunks):
            plain(token, chunk)
            if chunk:
                num, den = blend(token, chunk - 1, num, den)
        num_ref[...] = num
        den_ref[...] = den
        return carry

    def limit_squared():
        most = most_ref[...]
        most = (most * most).astype(jnp.bfloat16)
        twos = k2f[...]
        twos = (twos * twos).astype(jnp.bfloat16)
        ones = k1f[...]
        ones = (ones * ones).astype(jnp.bfloat16)
        over = (((1,), (1,)), ((), ()))
        left = lax.dot_general(most, twos, over, preferred_element_type=jnp.float32)
        right = lax.dot_general(
            ones, jnp.ones((depth, depth), jnp.bfloat16), over, preferred_element_type=jnp.float32
        )
        return 1.05 * jnp.max(left) * jnp.max(right)

    def shifted():
        load_keys(0)
        top = None
        for chunk in range(chunks):
            top = logits(0, chunk, top)
        lax.fori_loop(0, piece, step, top)

    def plainly():
        lax.fori_loop(0, piece, quick, 0, unroll=math.gcd(piece, UNROLL))

    small = limit_squared() < SAFE * SAFE

    @pl.when(small)
    def _():
        plainly()

    @pl.when(jnp.logical_not(small))
    def _():
        shifted()

    last_blend(piece - 1)


def body(queries, key_one, value_one, key_two, value_two):
    piece, heads, depth = queries.shape
    reach = (pieces_behind(WIN_ONE, piece), pieces_behind(WIN_TWO, piece))
    vmem = pl.BlockSpec(memory_space=pltpu.VMEM)
    inner = lax.axis_size("head")
    shards = shards_behind(reach[0], inner)
    slots = ((shards + 1) * inner, (shards + 1) * inner, reach[1] + 1, reach[1] + 1)
    long_one = (reach[0] * piece + depth, depth)
    long_two = (reach[1] * piece + depth, depth)
    made = pl.pallas_call(
        functools.partial(halo_kernel, reach),
        out_shape=[
            *[pltpu.VMEM((slot, piece, depth), key_one.dtype) for slot in slots],
            pltpu.VMEM(queries.shape, queries.dtype),
            pltpu.VMEM((piece + WIN_TWO - 2, depth, depth), jnp.float32),
            pltpu.VMEM((piece, depth), jnp.float32),
        ],
        in_specs=[pl.BlockSpec(memory_space=pltpu.HBM)] * 5,
        out_specs=[vmem] * 7,
        scratch_shapes=[
            *[pltpu.SemaphoreType.DMA((2, inner))] * 2,
            *[pltpu.SemaphoreType.DMA((2, shards, inner))] * 2,
            *[pltpu.SemaphoreType.DMA((2, reach[1]))] * 2,
            pltpu.SemaphoreType.DMA((5,)),
            pltpu.VMEM(((reach[1] + 1) * piece, depth), jnp.float32),
        ],
        compiler_params=pltpu.CompilerParams(
            collective_id=0, has_side_effects=True, vmem_limit_bytes=HALO_VMEM
        ),
    )(*[pltpu.with_memory_space_constraint(x, pltpu.HBM) for x in (queries, key_one, value_one, key_two, value_two)])
    made = [
        pltpu.with_memory_space_constraint(made[index], pltpu.VMEM) for index in (0, 1, 2, 3, 4, 5, 6)
    ]
    return pl.pallas_call(
        attend_kernel,
        out_shape=jax.ShapeDtypeStruct(queries.shape, queries.dtype),
        in_specs=[vmem] * 7,
        out_specs=vmem,
        scratch_shapes=[
            pltpu.VMEM(long_one, jnp.float32),
            pltpu.VMEM(long_one, jnp.float32),
            pltpu.VMEM(long_two, jnp.float32),
            pltpu.VMEM((WIN_ONE, depth), jnp.bfloat16),
            pltpu.VMEM((depth + 16, WIN_ONE), jnp.bfloat16),
            pltpu.VMEM((depth + 16, depth), jnp.float32),
            pltpu.VMEM((depth + 16, depth), jnp.float32),
            pltpu.VMEM((depth, depth), jnp.float32),
            pltpu.VMEM((8, depth), jnp.float32),
            pltpu.VMEM((WIN_TWO // LAG_CHUNK, WIN_ONE, LAG_CHUNK * heads), jnp.bfloat16),
            pltpu.VMEM((WIN_ONE, WIN_TWO * heads), jnp.float32),
        ],
        compiler_params=pltpu.CompilerParams(vmem_limit_bytes=ATTEND_VMEM),
    )(*made)


def solution(mesh):
    rows = P(("seq", "head"), None)
    placed = (P(("seq", "head"), None, None), rows, rows, rows, rows)
    return jax.shard_map(
        body, mesh=mesh, in_specs=placed, out_specs=P(("seq", "head"), None, None), check_vma=False
    )
```

```python
import functools
import math

import jax
import jax.numpy as jnp
from jax import lax
from jax.experimental import pallas as pl
from jax.experimental.pallas import tpu as pltpu
from jax.sharding import PartitionSpec as P

WIN_ONE = 512
WIN_TWO = 32
LAG_CHUNK = 8
ROW_L = 1
SAFE = 69.0
HALO_VMEM = 8 << 20
ATTEND_VMEM = 24 << 20
UNROLL = 20
HALF = 256


def pieces_behind(window, rows):
    return (window - 1) // rows + 1


def shards_behind(reach, inner):
    return (reach + inner - 1) // inner


def halo_kernel(reach, q, k1, v1, k2, v2, k1_out, v1_out, k2_out, v2_out, q_out, spread2, most, *rest):
    side_send, side_recv, fore_send, fore_recv, near_send, near_recv, local, v2f = rest
    inner, outer = lax.axis_size("head"), lax.axis_size("seq")
    seq, col = lax.axis_index("seq"), lax.axis_index("head")
    me, count = seq * inner + col, outer * inner
    shards = shards_behind(reach[0], inner)
    base = shards * inner
    firsts = ((k1, k1_out), (v1, v1_out))
    seconds = ((k2, k2_out), (v2, v2_out))

    def remote(source, target, send, recv, where):
        return pltpu.make_async_remote_copy(
            src_ref=source,
            dst_ref=target,
            send_sem=send,
            recv_sem=recv,
            device_id=where,
            device_id_type=pl.DeviceIdType.MESH,
        )

    def around(turn):
        other, bit = col, 1
        while bit < inner:
            if turn & bit:
                other = other + bit - 2 * bit * ((col // bit) % 2)
            bit = 2 * bit
        return other

    def side(turn):
        return [
            remote(
                target.at[base + col],
                target.at[base + col],
                side_send.at[flow, turn - 1],
                side_recv.at[flow, turn - 1],
                (seq, around(turn)),
            )
            for flow, (source, target) in enumerate(firsts)
        ]

    def side_arrival(turn):
        return [
            remote(
                target.at[base + around(turn)],
                target.at[base + around(turn)],
                side_send.at[flow, turn - 1],
                side_recv.at[flow, turn - 1],
                (seq, around(turn)),
            )
            for flow, (source, target) in enumerate(firsts)
        ]

    def fore(hop, turn):
        return [
            remote(
                target.at[base + around(turn)],
                target.at[(shards - hop) * inner + around(turn)],
                fore_send.at[flow, hop - 1, turn],
                fore_recv.at[flow, hop - 1, turn],
                (seq + hop, col),
            )
            for flow, (source, target) in enumerate(firsts)
        ]

    def near(step):
        there = me + step
        return [
            remote(
                target.at[reach[1]],
                target.at[reach[1] - step],
                near_send.at[flow, step - 1],
                near_recv.at[flow, step - 1],
                (there // inner, there % inner),
            )
            for flow, (source, target) in enumerate(seconds)
        ]

    def wanted(hop, turn):
        return hop * inner <= reach[0] + around(turn) - col

    def greet(where):
        pl.semaphore_signal(barrier, inc=1, device_id=where, device_id_type=pl.DeviceIdType.MESH)

    places = [base + col, base + col, reach[1], reach[1]]
    fetches = [
        pltpu.make_async_copy(source, target.at[place], local.at[index])
        for index, ((source, target), place) in enumerate(zip(firsts + seconds, places))
    ]
    fetches.append(pltpu.make_async_copy(q, q_out, local.at[4]))
    for fetch in fetches:
        fetch.start()
    barrier = pltpu.get_barrier_semaphore()
    hops = (reach[0] + inner - 1 - col) // inner
    for turn in range(1, inner):
        greet((seq, around(turn)))
    for hop in range(1, shards + 1):

        @pl.when((seq - hop >= 0) & (hop <= hops))
        def _():
            greet((seq - hop, col))

    for step in range(1, reach[1] + 1):

        @pl.when(me - step >= 0)
        def _():
            greet(((me - step) // inner, (me - step) % inner))

    peers = inner - 1 + jnp.minimum(hops, outer - 1 - seq) + jnp.minimum(reach[1], count - 1 - me)
    pl.semaphore_wait(barrier, peers)
    for fetch in fetches[:4]:
        fetch.wait()

    for turn in range(1, inner):
        for copy in side(turn):
            copy.start()
    for turn in range(inner):
        if turn:
            for copy in side_arrival(turn):
                copy.wait_recv()
        for hop in range(shards, 0, -1):

            @pl.when((seq + hop < outer) & wanted(hop, turn))
            def _():
                for copy in fore(hop, turn):
                    copy.start()

        if turn == 0:
            for step in range(1, reach[1] + 1):

                @pl.when(me + step < count)
                def _():
                    for copy in near(step):
                        copy.start()

    for step in range(1, reach[1] + 1):

        @pl.when(me - step >= 0)
        def _():
            for copy in near(step):
                copy.wait_recv()

    spread_tables(reach, me, v2_out, v2f, spread2, q_out.shape[1])
    fetches[4].wait()
    most[...] = jnp.max(jnp.abs(q_out[...].astype(jnp.float32)), axis=1)

    for turn in range(inner):
        for hop in range(shards, 0, -1):

            @pl.when((seq - hop >= 0) & wanted(hop, turn))
            def _():
                for copy in fore(hop, turn):
                    copy.wait_recv()

            @pl.when((seq + hop < outer) & wanted(hop, turn))
            def _():
                for copy in fore(hop, turn):
                    copy.wait_send()

    for step in range(1, reach[1] + 1):

        @pl.when(me + step < count)
        def _():
            for copy in near(step):
                copy.wait_send()

    for turn in range(1, inner):
        for copy in side(turn):
            copy.wait_send()


def spread_tables(reach, me, v2, v2f, spread2, heads):
    slots, piece, depth = v2.shape
    lead_two = reach[1] * piece
    for slot in range(slots):
        v2f[slot * piece : (slot + 1) * piece, :] = v2[slot].astype(jnp.float32)
    pos = lax.broadcasted_iota(jnp.int32, v2f.shape, 0)
    v2f[...] = jnp.where(pos < lead_two - me * piece, 0.0, v2f[...])
    lane = lax.broadcasted_iota(jnp.int32, (depth, depth), 1)
    sub = lax.broadcasted_iota(jnp.int32, (depth, depth), 0)
    own = jnp.where(lane == sub, 1.0, 0.0).astype(jnp.bfloat16)
    for index in range(0, spread2.shape[0], 2):
        rows = []
        for at in range(index, min(index + 2, spread2.shape[0])):
            row = lead_two - (WIN_TWO - 1) + at
            rows.append(jnp.broadcast_to(v2f[row + 1 : row + 2, :], (heads, depth)))
            rows.append(jnp.broadcast_to(v2f[row : row + 1, :], (heads, depth)))
        made = lax.dot_general(
            own,
            jnp.concatenate(rows, axis=0).astype(jnp.bfloat16),
            (((1,), (1,)), ((), ())),
            preferred_element_type=jnp.float32,
        )
        spread2[index] = made[:, :depth]
        if index + 1 < spread2.shape[0]:
            spread2[index + 1] = made[:, depth:]


def attend_kernel(*refs):
    k1h, v1h, k2h, v2h, q, spread2, most_ref, out = refs[:8]
    k1f, v1f, k2f, kw, vt, vold, vnew, num_ref, den_ref, raised, scores = refs[8:]
    piece, heads, depth = q.shape
    inner = lax.axis_size("head")
    reach = pieces_behind(WIN_ONE, piece)
    skip = lax.axis_index("head") + shards_behind(reach, inner) * inner - reach
    me = lax.axis_index("seq") * inner + lax.axis_index("head")
    lead_one = reach * piece
    lead_two = (k2h.shape[0] - 1) * piece
    scale = 1.0 / math.sqrt(depth)

    def spread(target, behind, skip, count):
        for slot in range(count):
            target[slot * piece : (slot + 1) * piece, :] = behind[skip + slot].astype(jnp.float32)
        if count * piece < target.shape[0]:
            target[count * piece :, :] = jnp.zeros((target.shape[0] - count * piece, depth), jnp.float32)

    spread(k1f, k1h, skip, reach + 1)
    spread(v1f, v1h, skip, reach + 1)
    spread(k2f, k2h, 0, k2h.shape[0])
    first_one = lead_one - me * piece
    first_two = lead_two - me * piece

    @pl.when(first_one > 0)
    def _():
        pos = lax.broadcasted_iota(jnp.int32, k1f.shape, 0)
        whole = k1f[...]
        head_row = jnp.sum(jnp.where(pos == first_one, whole, 0.0), axis=0, keepdims=True)
        k1f[...] = jnp.where(pos < first_one, head_row, whole)
        v1f[...] = jnp.where(pos < first_one, 0.0, v1f[...])

    pos_two = lax.broadcasted_iota(jnp.int32, k2f.shape, 0)
    whole_two = k2f[...]
    head_two = jnp.sum(jnp.where(pos_two == first_two, whole_two, 0.0), axis=0, keepdims=True)
    k2f[...] = jnp.where(pos_two < first_two, head_two, whole_two) * scale

    span = LAG_CHUNK * heads
    chunks = WIN_TWO // LAG_CHUNK
    start_one = lead_one - WIN_ONE
    fresh = -(-piece // 16) * 16
    lane = lax.broadcasted_iota(jnp.int32, (depth + 16, depth), 1)
    sub = lax.broadcasted_iota(jnp.int32, (depth + 16, depth), 0)
    row_f = lax.broadcasted_iota(jnp.int32, (fresh, depth), 0)

    kw[...] = k1f[start_one : start_one + WIN_ONE, :].astype(jnp.bfloat16)
    for lo in range(0, WIN_ONE, depth):
        turned = jnp.transpose(v1f[start_one + lo : start_one + lo + depth, :])
        valid = jnp.where(lane[depth:] + (start_one + lo) < first_one, 0.0, 1.0)
        made = jnp.concatenate([turned, valid], axis=0)
        if lo == 0:
            vold[...] = made
        else:
            vt[:, lo : lo + depth] = made.astype(jnp.bfloat16)
    vnew[...] = jnp.concatenate(
        [jnp.transpose(v1f[lead_one : lead_one + depth, :]), jnp.ones((16, depth), jnp.float32)], axis=0
    )

    def load_keys(token):
        head = jnp.where(row_f <= token, k1f[lead_one : lead_one + fresh, :], k1f[start_one : start_one + fresh, :])
        kw[:fresh, :] = head.astype(jnp.bfloat16)

    def load_values(token):
        vt[:, :depth] = jnp.where(lane <= token, vnew[...], vold[...]).astype(jnp.bfloat16)

    behind_two = WIN_TWO - 1

    def products(token, chunk):
        query = q[token].astype(jnp.float32)
        rows = []
        for lag in range(chunk * LAG_CHUNK, (chunk + 1) * LAG_CHUNK):
            near = k2f[pl.ds(lead_two + token - lag, 1), :]
            rows.append((query * near).astype(jnp.bfloat16))
        return jnp.concatenate(rows, axis=0)

    def logits(token, chunk, top):
        product = products(token, chunk)
        for lo in range(0, WIN_ONE, WIN_ONE // ROW_L):
            made = lax.dot_general(
                kw[lo : lo + WIN_ONE // ROW_L, :],
                product,
                (((1,), (1,)), ((), ())),
                preferred_element_type=jnp.float32,
            )
            scores[lo : lo + WIN_ONE // ROW_L, chunk * span : (chunk + 1) * span] = made
            best = jnp.max(made.reshape(WIN_ONE // ROW_L // 8, 8, span), axis=0)
            parts = [best[:, at : at + depth] for at in range(0, span, depth)]
            top = parts if top is None else [jnp.maximum(a, b) for a, b in zip(top, parts)]
        return top

    num_ref[...] = jnp.zeros(num_ref.shape, jnp.float32)
    den_ref[...] = jnp.ones(den_ref.shape, jnp.float32)

    def finish(token, num, den):
        den = den + pltpu.roll(den, heads, 1)
        inverse = 1.0 / den
        num = num.reshape(depth // 8, 8, depth) * inverse[None]
        turned = jnp.transpose(num.reshape(depth, depth))
        out[token] = (turned[:heads] + turned[heads:]).astype(out.dtype)

    def weigh(chunk, peak):
        parts = scores[:, chunk * span : (chunk + 1) * span].reshape(WIN_ONE // 8, 8, span)
        raised[chunk] = jnp.exp(parts - peak[None]).astype(jnp.bfloat16).reshape(WIN_ONE, span)

    def blend(token, chunk, num, den):
        mixed = jnp.dot(vt[...], raised[chunk], preferred_element_type=jnp.float32)
        return gather(token, chunk, mixed, num, den)

    def gather(token, chunk, mixed, num, den):
        for at in range(0, span, depth):
            lag = chunk * LAG_CHUNK + at // heads
            more = mixed[:depth, at : at + depth] * spread2[token - lag + behind_two - 1]
            known = jnp.where(lane[:8] // heads + (lag - token) <= me * piece, 1.0, 0.0)
            count = mixed[depth : depth + 8, at : at + depth] * known
            num = more if num is None else num + more
            den = count if den is None else den + count
        return num, den

    def last_blend(token):
        num, den = blend(token, chunks - 1, num_ref[...], den_ref[...])
        finish(token, num, den)

    def step(token, top):
        later = jnp.minimum(token + 1, piece - 1)
        peak = jnp.max(functools.reduce(jnp.maximum, top), axis=0, keepdims=True)
        peak = jnp.broadcast_to(jnp.maximum(peak, pltpu.roll(peak, heads, 1)), (8, depth))
        peak = jnp.concatenate([peak] * (span // depth), axis=1)
        last_blend(jnp.maximum(token - 1, 0))
        load_values(token)
        load_keys(later)
        num = den = later_top = None
        for chunk in range(chunks):
            if chunk:
                num, den = blend(token, chunk - 1, num, den)
            weigh(chunk, peak)
            later_top = logits(later, chunk, later_top)
        num_ref[...] = num
        den_ref[...] = den
        return later_top

    def plain(token, chunk, at, product):
        raised[chunk, at : at + HALF] = jnp.exp(
            lax.dot_general(
                kw[at : at + HALF], product, (((1,), (1,)), ((), ())), preferred_element_type=jnp.float32
            )
        ).astype(jnp.bfloat16)

    def half_blend(token, chunk, at, num, den):
        mixed = jnp.dot(vt[:, at : at + HALF], raised[chunk, at : at + HALF], preferred_element_type=jnp.float32)
        return gather(token, chunk, mixed, num, den)

    def quick(token, carry):
        num, den = num_ref[...], den_ref[...]
        before = jnp.maximum(token - 1, 0)
        product = products(token, 0)
        load_keys(token)
        for at in range(0, WIN_ONE, HALF):
            plain(token, 0, at, product)
            num, den = half_blend(before, chunks - 1, at, num, den)
        finish(before, num, den)
        load_values(token)
        num = den = None
        for chunk in range(1, chunks):
            product = products(token, chunk)
            for at in range(0, WIN_ONE, HALF):
                plain(token, chunk, at, product)
                num, den = half_blend(token, chunk - 1, at, num, den)
        num_ref[...] = num
        den_ref[...] = den
        return carry

    def limit_squared():
        most = most_ref[...]
        most = (most * most).astype(jnp.bfloat16)
        twos = k2f[...]
        twos = (twos * twos).astype(jnp.bfloat16)
        ones = k1f[...]
        ones = (ones * ones).astype(jnp.bfloat16)
        over = (((1,), (1,)), ((), ()))
        left = lax.dot_general(most, twos, over, preferred_element_type=jnp.float32)
        right = lax.dot_general(
            ones, jnp.ones((depth, depth), jnp.bfloat16), over, preferred_element_type=jnp.float32
        )
        return 1.05 * jnp.max(left) * jnp.max(right)

    def shifted():
        load_keys(0)
        top = None
        for chunk in range(chunks):
            top = logits(0, chunk, top)
        lax.fori_loop(0, piece, step, top)

    def plainly():
        lax.fori_loop(0, piece, quick, 0, unroll=math.gcd(piece, UNROLL))

    small = limit_squared() < SAFE * SAFE

    @pl.when(small)
    def _():
        plainly()

    @pl.when(jnp.logical_not(small))
    def _():
        shifted()

    last_blend(piece - 1)


def body(queries, key_one, value_one, key_two, value_two):
    piece, heads, depth = queries.shape
    reach = (pieces_behind(WIN_ONE, piece), pieces_behind(WIN_TWO, piece))
    vmem = pl.BlockSpec(memory_space=pltpu.VMEM)
    inner = lax.axis_size("head")
    shards = shards_behind(reach[0], inner)
    slots = ((shards + 1) * inner, (shards + 1) * inner, reach[1] + 1, reach[1] + 1)
    long_one = (reach[0] * piece + depth, depth)
    long_two = (reach[1] * piece + depth, depth)
    made = pl.pallas_call(
        functools.partial(halo_kernel, reach),
        out_shape=[
            *[pltpu.VMEM((slot, piece, depth), key_one.dtype) for slot in slots],
            pltpu.VMEM(queries.shape, queries.dtype),
            pltpu.VMEM((piece + WIN_TWO - 2, depth, depth), jnp.float32),
            pltpu.VMEM((piece, depth), jnp.float32),
        ],
        in_specs=[pl.BlockSpec(memory_space=pltpu.HBM)] * 5,
        out_specs=[vmem] * 7,
        scratch_shapes=[
            *[pltpu.SemaphoreType.DMA((2, inner))] * 2,
            *[pltpu.SemaphoreType.DMA((2, shards, inner))] * 2,
            *[pltpu.SemaphoreType.DMA((2, reach[1]))] * 2,
            pltpu.SemaphoreType.DMA((5,)),
            pltpu.VMEM(((reach[1] + 1) * piece, depth), jnp.float32),
        ],
        compiler_params=pltpu.CompilerParams(
            collective_id=0, has_side_effects=True, vmem_limit_bytes=HALO_VMEM
        ),
    )(*[pltpu.with_memory_space_constraint(x, pltpu.HBM) for x in (queries, key_one, value_one, key_two, value_two)])
    made = [
        pltpu.with_memory_space_constraint(made[index], pltpu.VMEM) for index in (0, 1, 2, 3, 4, 5, 6)
    ]
    return pl.pallas_call(
        attend_kernel,
        out_shape=jax.ShapeDtypeStruct(queries.shape, queries.dtype),
        in_specs=[vmem] * 7,
        out_specs=vmem,
        scratch_shapes=[
            pltpu.VMEM(long_one, jnp.float32),
            pltpu.VMEM(long_one, jnp.float32),
            pltpu.VMEM(long_two, jnp.float32),
            pltpu.VMEM((WIN_ONE, depth), jnp.bfloat16),
            pltpu.VMEM((depth + 16, WIN_ONE), jnp.bfloat16),
            pltpu.VMEM((depth + 16, depth), jnp.float32),
            pltpu.VMEM((depth + 16, depth), jnp.float32),
            pltpu.VMEM((depth, depth), jnp.float32),
            pltpu.VMEM((8, depth), jnp.float32),
            pltpu.VMEM((WIN_TWO // LAG_CHUNK, WIN_ONE, LAG_CHUNK * heads), jnp.bfloat16),
            pltpu.VMEM((WIN_ONE, WIN_TWO * heads), jnp.float32),
        ],
        compiler_params=pltpu.CompilerParams(vmem_limit_bytes=ATTEND_VMEM),
    )(*made)


def solution(mesh):
    rows = P(("seq", "head"), None)
    placed = (P(("seq", "head"), None, None), rows, rows, rows, rows)
    return jax.shard_map(
        body, mesh=mesh, in_specs=placed, out_specs=P(("seq", "head"), None, None), check_vma=False
    )
```
